128 devices in a mesh: dp: 8 (over y, z_hi), proto: 16 (over z_lo, x, core).
Axes of the slice: x: 4, y: 4, z: 4 (z_hi: 2, z_lo: 2; z = z_hi * 2 + z_lo), core: 2. Of those that a mesh axis runs over, the one named last changes fastest.
Arguments:
- student_patch: bfloat16 [8, 2048, 256], P('dp', 'proto'), may hold values from -4 to 4
- teacher_patch: bfloat16 [8, 2048, 256], P('dp', 'proto'), may hold values from -4 to 4
- patch_image: int32 [8, 2048], P('dp', 'proto'), may hold values from 0 to 7, never falling along the last dimension, each value on 1 to 512 neighbouring positions
- masked_rows: int32 [8, 1024], P('dp', 'proto'), may hold values from 0 to 127, as said below
- student_proto: float32 [256, 131072], P(None, 'proto'), as said below
- teacher_proto: float32 [256, 131072], P(None, 'proto'), as said below
- first_moment: float32 [256, 131072], P('dp', 'proto'), as said below
- second_moment: float32 [256, 131072], P('dp', 'proto'), as said below
- centre: float32 [131072], P('proto'), may hold values from -0.3 to 0.3
Outputs:
- row_grad: float32 [8, 1024, 256], P('dp', 'proto')
- new_student: float32 [256, 131072], P('dp', 'proto')
- new_first: float32 [256, 131072], P('dp', 'proto')
- new_second: float32 [256, 131072], P('dp', 'proto')
- new_teacher: float32 [256, 131072], P('dp', 'proto')
- loss: float32 [], replicated
The draws below stay inside these ranges and needn't reach their ends.
Inputs may be any that keep to these rules, and one draw needn't show every extreme that they name: `masked_rows`: for each data group and each index of proto in order, 64 distinct positions among that device's 128 patches, ascending; position 0 and position 127 of every device are always masked. `student_proto`: finite entries. `teacher_proto`: finite entries. `first_moment`: finite entries. `second_moment`: positive entries.
All inputs are finite; a program needn't handle non-finite values.
Results may differ from the reference program's by a relative error of at most 0.014.
Values may be sent and summed in bfloat16 or wider, within the bound.
A program may use at most 256 MiB of HBM per device.

```python
import math
import jax
import jax.numpy as jnp
import numpy as np
from jax import lax

E = 256
K = 131072
MASK_DEV = 64
PATCH_IMG = 256
PATCH_DEV = 128
ROWS_GROUP = 1024
ROWS = 8192
IMG_GROUP = 8
IMAGES = 64
K_DEV = 8192
N_DP = 8
N_PROTO = 16


def group_mix():
    place = jnp.arange(N_DP, dtype=jnp.float32) / max(N_DP - 1, 1)
    return 0.95 * place


def common_noise(key):
    return jax.random.normal(jax.random.fold_in(key, 11), (N_DP, PATCH_DEV * N_PROTO, E), jnp.float32)


def student_rows(key):
    values = common_noise(key)
    return jnp.clip(values, -4.0, 4.0)


def teacher_rows(key):
    subkey = jax.random.fold_in(key, 12)
    own = jnp.clip(jax.random.normal(subkey, (N_DP, PATCH_DEV * N_PROTO, E), jnp.float32), -1.5, 1.5)
    mix = group_mix()[:, None, None]
    values = mix * common_noise(key) + jnp.sqrt(1.0 - mix * mix) * own
    return jnp.clip(values, -4.0, 4.0)


def column_scale(key):
    phase = jax.random.uniform(jax.random.fold_in(key, 23), (), jnp.float32, 0.0, 2.0 * math.pi)
    place = jnp.arange(K, dtype=jnp.float32) / K
    return jnp.exp(0.25 * jnp.sin(2.0 * math.pi * place + phase))


def base_table(key):
    table = jnp.clip(jax.random.normal(jax.random.fold_in(key, 21), (E, K), jnp.float32), -4.0, 4.0)
    return table * 0.0625 * column_scale(key)[None, :]


def add_spikes(table):
    return table


def grad_scale():
    return 20.0 * math.sqrt(ROWS) / (K * math.sqrt(E))


def draw_student_patch(key, part):
    return student_rows(key).astype(jnp.bfloat16)


def draw_teacher_patch(key, part):
    return teacher_rows(key).astype(jnp.bfloat16)


def draw_student_proto(key, part):
    return add_spikes(base_table(key))


def draw_teacher_proto(key, part):
    drift = jnp.clip(jax.random.normal(jax.random.fold_in(key, 22), (E, K), jnp.float32), -3.0, 3.0) * 0.0125
    return add_spikes(base_table(key) + drift)


def draw_centre(key, part):
    phase = jax.random.uniform(jax.random.fold_in(key, 51), (), jnp.float32, 0.0, 2.0 * math.pi)
    place = jnp.arange(K, dtype=jnp.float32) / K
    subkey = jax.random.fold_in(key, 52)
    amplitude = 0.5
    rough = jnp.clip(jax.random.normal(subkey, (K,), jnp.float32), -3.0, 3.0) * 0.02
    values = 0.07 * amplitude * jnp.sin(2.0 * math.pi * place + phase) + rough
    return values


def draw_masked_rows(key, part):
    device_keys = jax.random.split(jax.random.fold_in(key, 31), N_DP * N_PROTO)

    def one_device(device_key):
        middle = jax.random.permutation(device_key, PATCH_DEV - 2).astype(jnp.int32) + 1
        chosen = jnp.concatenate([jnp.zeros((1,), jnp.int32), middle[:MASK_DEV - 2], jnp.full((1,), PATCH_DEV - 1, jnp.int32)])
        return jnp.sort(chosen).astype(jnp.int32)
    picked = jax.vmap(one_device)(device_keys)
    return picked.reshape(N_DP, N_PROTO * MASK_DEV).astype(jnp.int32)


def draw_first_moment(key, part):
    subkey = jax.random.fold_in(key, 41)
    values = jnp.clip(jax.random.normal(subkey, (E, K), jnp.float32), -5.0, 5.0) * 0.25
    return values * grad_scale()


def draw_second_moment(key, part):
    subkey = jax.random.fold_in(key, 42)
    spread = jax.random.uniform(subkey, (E, K), jnp.float32, math.log(0.25), math.log(4.0))
    return jnp.exp(spread) * (0.095 * grad_scale() * grad_scale())


def profile(number_of, total, reach, lean):
    portions = [(1 << 20) // math.isqrt(grade ** lean) + 1 for grade in range(2, number_of + 1)]
    spare, given = total - reach - (number_of - 1), [1] * (number_of - 1)
    while spare > 0:
        candidates = [i for i in range(number_of - 1) if given[i] < reach]
        mass, left = sum([portions[i] for i in candidates]), spare
        for i in candidates:
            extra = min(reach - given[i], max(1, left * portions[i] // mass), spare)
            given[i] = given[i] + extra
            spare = spare - extra
    return np.array([reach] + given)


def ragged_sizes(own_key, amount, total, most, slope):
    if amount == 2:
        one = jax.random.randint(own_key, (), max(1, total - most), min(most, total - 1) + 1)
        return jnp.stack([one, total - one])
    tallies = jnp.asarray(profile(amount, total, most, slope), jnp.int32)
    couples = (amount - 1) // 2
    source_of, receiver = tallies[1:1 + 2 * couples:2], tallies[2:2 + 2 * couples:2]
    slack = jnp.minimum(source_of - 1, most - receiver)
    passed = jax.random.randint(jax.random.fold_in(own_key, 1), (couples,), 0, 1 << 20) % (slack + 1)
    tallies = tallies.at[1:1 + 2 * couples:2].set(source_of - passed).at[2:2 + 2 * couples:2].set(receiver + passed)
    return tallies[jax.random.permutation(jax.random.fold_in(own_key, 2), amount)]


def setup_inputs(seed: int = 0) -> dict:
    key_of = jax.random.split(jax.random.key(seed), 10)
    return {
        "student_patch": draw_student_patch(jax.random.fold_in(key_of[9], 71), 0),
        "teacher_patch": draw_teacher_patch(jax.random.fold_in(key_of[9], 71), 0),
        "patch_image": jax.vmap(lambda own: jnp.searchsorted(jnp.cumsum(ragged_sizes(own, IMG_GROUP, PATCH_DEV * N_PROTO, 2 * PATCH_IMG, 1)), jnp.arange(PATCH_DEV * N_PROTO), side="right"))(jax.random.split(key_of[2], N_DP)).reshape((N_DP, PATCH_DEV * N_PROTO)).astype(jnp.int32),
        "masked_rows": draw_masked_rows(jax.random.fold_in(key_of[9], 71), 0),
        "student_proto": draw_student_proto(jax.random.fold_in(key_of[9], 71), 0),
        "teacher_proto": draw_teacher_proto(jax.random.fold_in(key_of[9], 71), 0),
        "first_moment": draw_first_moment(jax.random.fold_in(key_of[9], 71), 0),
        "second_moment": draw_second_moment(jax.random.fold_in(key_of[9], 71), 0),
        "centre": draw_centre(jax.random.fold_in(key_of[9], 71), 0),
    }


student_temp = 0.1
teacher_temp = 0.07
beta_one = 0.9
beta_two = 0.999
fix_one = 0.9999734386011124
fix_two = 0.09520785288629038
learn_rate = 0.002
decay_rate = 0.04
teacher_keep = 0.994

def unit_rows(raw_rows):
    inverse = lax.rsqrt(lax.optimization_barrier(jnp.sum(raw_rows * raw_rows, axis=-1, keepdims=True)) + 1e-06)
    return (raw_rows * inverse, inverse)

def reference(student_patch, teacher_patch, patch_image, masked_rows, student_proto, teacher_proto, first_moment, second_moment, centre):
    offsets = (jnp.arange(ROWS_GROUP, dtype=jnp.int32) // MASK_DEV * PATCH_DEV).astype(jnp.int32)
    places = (masked_rows + offsets[None, :]).astype(jnp.int32)
    pick_rows = jax.vmap(lambda patch_table, row_where: patch_table[row_where])
    raw_student = pick_rows(student_patch, places).astype(jnp.float32)
    raw_teacher = pick_rows(teacher_patch, places).astype(jnp.float32)
    image_ids = pick_rows(patch_image, places)
    unit_student, inv_student = unit_rows(raw_student)
    unit_teacher, inv_teacher = unit_rows(raw_teacher)
    rows_student = unit_student.astype(jnp.bfloat16).reshape(ROWS, E)
    rows_teacher = unit_teacher.astype(jnp.bfloat16).reshape(ROWS, E)
    labels = jnp.arange(IMG_GROUP, dtype=jnp.int32)
    matches = (image_ids[:, :, None] == labels[None, None, :]).astype(jnp.float32)
    counts = lax.optimization_barrier(jnp.sum(matches, axis=1))
    per_row = jnp.einsum('gri,gi->gr', matches, counts, precision=lax.Precision.HIGHEST)
    weights = (ROWS / IMAGES / per_row).reshape(ROWS)
    student_w = student_proto.astype(jnp.bfloat16)
    teacher_w = teacher_proto.astype(jnp.bfloat16)

    def logits(block_index):
        first_col = block_index * K_DEV
        ws_block = lax.dynamic_slice_in_dim(student_w, first_col, K_DEV, 1)
        wt_block = lax.dynamic_slice_in_dim(teacher_w, first_col, K_DEV, 1)
        centre_block = lax.dynamic_slice_in_dim(centre, first_col, K_DEV, 0)
        student_logit = jnp.dot(rows_student, ws_block, preferred_element_type=jnp.float32) / student_temp
        teacher_raw = jnp.dot(rows_teacher, wt_block, preferred_element_type=jnp.float32)
        teacher_logit = (teacher_raw - centre_block) / teacher_temp
        return (student_logit, teacher_logit, ws_block)

    def first_pass(state_in, block_index):
        peak_s, sum_s, peak_t, sum_t = state_in
        student_logit, teacher_logit, ws_block = logits(block_index)
        new_peak_s = jnp.maximum(peak_s, lax.optimization_barrier(jnp.max(student_logit, axis=1)))
        new_peak_t = jnp.maximum(peak_t, lax.optimization_barrier(jnp.max(teacher_logit, axis=1)))
        sum_s = sum_s * jnp.exp(peak_s - new_peak_s) + lax.optimization_barrier(jnp.sum(jnp.exp(student_logit - new_peak_s[:, None]), axis=1))
        sum_t = sum_t * jnp.exp(peak_t - new_peak_t) + lax.optimization_barrier(jnp.sum(jnp.exp(teacher_logit - new_peak_t[:, None]), axis=1))
        return ((new_peak_s, sum_s, new_peak_t, sum_t), None)
    lowest = jnp.full((ROWS,), -jnp.inf, jnp.float32)
    nothing = jnp.zeros((ROWS,), jnp.float32)
    block_ids = jnp.arange(N_PROTO, dtype=jnp.int32)
    (peak_s, sum_s, peak_t, sum_t), unused = lax.scan(first_pass, (lowest, nothing, lowest, nothing), block_ids)
    log_total = peak_s + jnp.log(sum_s)

    def second_pass(state_in, block_index):
        loss_acc, unit_grad = state_in
        student_logit, teacher_logit, ws_block = logits(block_index)
        prob_s = jnp.exp(student_logit - peak_s[:, None]) / sum_s[:, None]
        prob_t = jnp.exp(teacher_logit - peak_t[:, None]) / sum_t[:, None]
        loss_acc = loss_acc + jnp.sum(weights * lax.optimization_barrier(jnp.sum(prob_t * (log_total[:, None] - student_logit), axis=1)))
        grad_logit = (weights[:, None] * (prob_s - prob_t) / student_temp).astype(jnp.bfloat16)
        unit_grad = unit_grad + lax.dot_general(grad_logit, ws_block, (((1,), (1,)), ((), ())), preferred_element_type=jnp.float32)
        partial_value = jnp.einsum('gre,grk->gek', rows_student.reshape(N_DP, ROWS_GROUP, E).astype(jnp.float32), grad_logit.reshape(N_DP, ROWS_GROUP, K_DEV).astype(jnp.float32))
        rounded = lax.optimization_barrier(partial_value.astype(jnp.bfloat16))
        return ((loss_acc, unit_grad), lax.optimization_barrier(jnp.sum(rounded.astype(jnp.float32), axis=0)))
    start_state = (jnp.zeros((), jnp.float32), jnp.zeros((ROWS, E), jnp.float32))
    (loss_acc, unit_grad), grad_parts = lax.scan(second_pass, start_state, block_ids)
    proto_grad = jnp.transpose(grad_parts, (1, 0, 2)).reshape(E, K)
    unit_grad = unit_grad.reshape(N_DP, ROWS_GROUP, E)
    row_grad = inv_student * unit_grad - inv_student * inv_student * inv_student * raw_student * lax.optimization_barrier(jnp.sum(raw_student * unit_grad, axis=-1, keepdims=True))
    new_first = beta_one * first_moment + (1.0 - beta_one) * proto_grad
    new_second = beta_two * second_moment + (1.0 - beta_two) * proto_grad * proto_grad
    step_size = new_first / fix_one / (jnp.sqrt(new_second / fix_two) + 1e-08)
    new_student = student_proto - learn_rate * (step_size + decay_rate * student_proto)
    new_teacher = teacher_keep * teacher_proto + (1.0 - teacher_keep) * new_student
    loss = loss_acc / ROWS
    return (row_grad, new_student, new_first, new_second, new_teacher, loss)
```

```python
import functools
import math

import jax
import jax.numpy as jnp
from jax import lax
from jax.experimental import pallas as pl
from jax.experimental.pallas import tpu as pltpu
from jax.sharding import PartitionSpec as P

PATCH_IMG = 256
IMG_GROUP = 8

student_temp = 0.1
teacher_temp = 0.07
beta_one = 0.9
beta_two = 0.999
fix_one = 0.9999734386011124
fix_two = 0.09520785288629038
learn_rate = 0.002
decay_rate = 0.04
teacher_keep = 0.994

F32 = jnp.float32
BF16 = jnp.bfloat16
MESH = pl.DeviceIdType.MESH
LOG2E = math.log2(math.e)
LN2 = math.log(2.0)
SCALE_S = LOG2E / student_temp
SCALE_T = LOG2E / teacher_temp
LOWEST = -3.0e38
LANES = 128


def iota(shape, axis):
    return lax.broadcasted_iota(jnp.int32, shape, axis)


def eye(n):
    return iota((n, n), 0) == iota((n, n), 1)


def to_column(row):
    n = row.shape[1]
    return jnp.sum(jnp.where(eye(n), jnp.broadcast_to(row, (n, n)), 0.0), axis=1, keepdims=True)


def to_row(column):
    n = column.shape[0]
    return jnp.sum(jnp.where(eye(n), jnp.broadcast_to(column, (n, n)), 0.0), axis=0, keepdims=True)


def head_kernel(
    n_dp,
    n_proto,
    student_patch,
    teacher_patch,
    patch_image,
    masked_rows,
    student_hbm,
    teacher_hbm,
    centre,
    row_grad_out,
    proto_grad_out,
    loss_out,
    stage,
    ws,
    wt,
    rows,
    rows_across,
    raw_keep,
    inv_keep,
    ids,
    peak_s,
    sum_s,
    peak_t,
    sum_t,
    weight_tile,
    lse_send,
    lse_all,
    unit_acc,
    unit_send,
    unit_recv,
    slab_send,
    slab_recv,
    loss_send,
    loss_recv,
    group_send,
    group_recv,
    stage_sem,
    row_ssem,
    row_rsem,
    id_ssem,
    id_rsem,
    lse_ssem,
    lse_rsem,
    unit_ssem,
    unit_rsem,
    slab_ssem,
    slab_rsem,
    loss_ssem,
    loss_rsem,
    group_ssem,
    group_rsem,
):
    d = lax.axis_index("dp")
    p = lax.axis_index("proto")
    mask_count = masked_rows.shape[1]
    patch_count = patch_image.shape[1]
    emb, cols = ws.shape
    n_rows = rows.shape[0]
    slab = emb // n_dp
    load_cols = stage.shape[2]
    row_chunk = 256
    n_groups = n_rows // LANES

    def proto_peer(i):
        return lax.rem(p + i, n_proto)

    def dp_peer(i):
        return lax.rem(d + i, n_dp)

    def push(src, dst, ssem, rsem, target):
        return pltpu.make_async_remote_copy(
            src_ref=src, dst_ref=dst, send_sem=ssem, recv_sem=rsem, device_id=target, device_id_type=MESH
        )

    barrier = pltpu.get_barrier_semaphore()
    for i in range(1, n_proto):
        pl.semaphore_signal(barrier, inc=1, device_id=(d, proto_peer(i)), device_id_type=MESH)
    for i in range(1, n_dp):
        pl.semaphore_signal(barrier, inc=1, device_id=(dp_peer(i), p), device_id_type=MESH)

    n_load = cols // load_cols
    n_buf = stage.shape[0]

    def load(hbm, j, slot):
        c0 = pl.multiple_of(j * load_cols, load_cols)
        return pltpu.make_async_copy(hbm.at[:, pl.ds(c0, load_cols)], stage.at[slot], stage_sem.at[slot])

    load(student_hbm, 0, 0).start()
    load(teacher_hbm, 0, 1).start()
    load(student_hbm, 1, 2).start()
    load(teacher_hbm, 1, 3).start()

    picked = to_column(masked_rows[...].astype(F32))
    one_hot = iota((mask_count, patch_count), 1).astype(F32) == picked
    one_hot_f = jnp.where(one_hot, 1.0, 0.0)
    one_hot_b = one_hot_f.astype(BF16)
    own = pl.ds(pl.multiple_of(p * mask_count, mask_count), mask_count)
    raw_s = jnp.dot(one_hot_b, student_patch[...], preferred_element_type=F32)
    raw_t = jnp.dot(one_hot_b, teacher_patch[...], preferred_element_type=F32)
    inv_s = lax.rsqrt(jnp.sum(raw_s * raw_s, axis=1, keepdims=True) + 1e-06)
    inv_t = lax.rsqrt(jnp.sum(raw_t * raw_t, axis=1, keepdims=True) + 1e-06)
    rows[own, :emb] = (raw_s * inv_s).astype(BF16)
    rows[own, emb:] = (raw_t * inv_t).astype(BF16)
    raw_keep[...] = raw_s
    inv_keep[...] = jnp.broadcast_to(inv_s, inv_keep.shape)
    own_ids = to_row(jnp.sum(one_hot_f * patch_image[...].astype(F32), axis=1, keepdims=True))
    ids[p] = jnp.broadcast_to(jnp.concatenate([own_ids, own_ids], axis=1), (8, LANES))

    pl.semaphore_wait(barrier, n_proto + n_dp - 2)

    def block_of(q):
        return rows.at[pl.ds(pl.multiple_of(q * mask_count, mask_count), mask_count)]

    twin = p + 1 - 2 * lax.rem(p, 2)
    sends = []
    for i in range(2, n_proto, 2):
        sends.append(push(block_of(p), block_of(p), row_ssem.at[i], row_rsem.at[p], (d, proto_peer(i))))
    sends.append(push(block_of(p), block_of(p), row_ssem.at[0], row_rsem.at[p], (d, twin)))
    for i in range(1, n_proto):
        sends.append(push(ids.at[p], ids.at[p], id_ssem.at[i], id_rsem.at[p], (d, proto_peer(i))))
    for copy in sends:
        copy.start()

    def cast_step(j, carry):
        c0 = pl.multiple_of(j * load_cols, load_cols)
        odd = lax.rem(j, 2) * 2
        load(student_hbm, j, odd).wait()
        ws[:, pl.ds(c0, load_cols)] = stage[odd].astype(BF16)

        @pl.when(j + 2 < n_load)
        def _():
            load(student_hbm, j + 2, odd).start()

        load(teacher_hbm, j, odd + 1).wait()
        wt[:, pl.ds(c0, load_cols)] = stage[odd + 1].astype(BF16)

        @pl.when(j + 2 < n_load)
        def _():
            load(teacher_hbm, j + 2, odd + 1).start()

        return carry

    lax.fori_loop(0, n_load, cast_step, 0)

    forwards = []
    for i in range(2, n_proto, 2):
        q = lax.rem(p + n_proto - i, n_proto)
        push(block_of(q), block_of(q), row_ssem.at[i], row_rsem.at[q], (d, twin)).wait_recv()
        forward = push(block_of(q), block_of(q), row_ssem.at[i + 1], row_rsem.at[q], (d, twin))
        forward.start()
        forwards.append(forward)
    push(block_of(twin), block_of(twin), row_ssem.at[0], row_rsem.at[twin], (d, twin)).wait_recv()
    for i in range(2, n_proto, 2):
        q = lax.rem(twin + n_proto - i, n_proto)
        push(block_of(q), block_of(q), row_ssem.at[i], row_rsem.at[q], (d, twin)).wait_recv()
    for i in range(1, n_proto):
        q = lax.rem(p + n_proto - i, n_proto)
        push(ids.at[q], ids.at[q], id_ssem.at[i], id_rsem.at[q], (d, twin)).wait_recv()

    lane = iota((1, LANES), 1)
    id_rows = [
        jnp.where(lane < mask_count, ids[2 * g, 0:1, :], ids[2 * g + 1, 0:1, :]) for g in range(n_groups)
    ]
    id_tile = jnp.concatenate(id_rows, axis=0)
    weight = jnp.zeros_like(id_tile)
    row_ratio = float(mask_count * PATCH_IMG // patch_count)
    for label in range(IMG_GROUP):
        match = id_tile == float(label)
        hits = jnp.where(match, 1.0, 0.0)
        count = jnp.sum(jnp.sum(hits, axis=0, keepdims=True), axis=1, keepdims=True)
        weight = weight + hits * (row_ratio / jnp.maximum(count, 1.0))
    weight_tile[...] = weight

    for peak, total in ((peak_s, sum_s), (peak_t, sum_t)):
        peak[...] = jnp.full(peak.shape, LOWEST, F32)
        total[...] = jnp.zeros(total.shape, F32)
    cols_one = 512

    def first_step(j, carry):
        c0 = pl.multiple_of(j * cols_one, cols_one)
        for r in range(n_rows // row_chunk):
            part = slice(r * row_chunk, (r + 1) * row_chunk)
            for e0, w, peak, total, scale, shift in (
                (0, ws, peak_s, sum_s, SCALE_S, False),
                (emb, wt, peak_t, sum_t, SCALE_T, True),
            ):
                z = jnp.dot(rows[part, e0 : e0 + emb], w[:, pl.ds(c0, cols_one)], preferred_element_type=F32)
                if shift:
                    z = z - centre[:, pl.ds(c0, cols_one)]
                pieces = [z[:, k * LANES : (k + 1) * LANES] for k in range(cols_one // LANES)]
                before = peak[part, :]
                now = before
                for piece in pieces:
                    now = jnp.maximum(now, piece)
                acc = total[part, :] * jnp.exp2((before - now) * scale)
                for piece in pieces:
                    acc = acc + jnp.exp2((piece - now) * scale)
                total[part, :] = acc
                peak[part, :] = now
        return carry

    lax.fori_loop(0, cols // cols_one, first_step, 0)

    for k, (peak, total, scale) in enumerate(((peak_s, sum_s, SCALE_S), (peak_t, sum_t, SCALE_T))):
        for g in range(n_groups):
            part = slice(g * LANES, (g + 1) * LANES)
            lanes_peak = peak[part, :]
            top = jnp.max(lanes_peak, axis=1, keepdims=True)
            mass = jnp.sum(total[part, :] * jnp.exp2((lanes_peak - top) * scale), axis=1, keepdims=True)
            r = k * n_groups + g
            lse_send[r : r + 1, :] = to_row(top * scale + jnp.log(mass) * LOG2E)
    lse_all[p] = lse_send[...]
    lse_copies = []
    for i in range(1, n_proto):
        lse_copies.append(
            push(lse_send, lse_all.at[p], lse_ssem.at[i], lse_rsem.at[p], (d, proto_peer(i)))
        )
    for copy in lse_copies:
        copy.start()

    rows_across[...] = rows[:, :emb].T
    unit_acc[...] = jnp.zeros(unit_acc.shape, F32)

    for i in range(1, n_proto):
        q = lax.rem(p + n_proto - i, n_proto)
        push(lse_send, lse_all.at[q], lse_ssem.at[i], lse_rsem.at[q], (d, twin)).wait_recv()
    top = lse_all[0]
    for q in range(1, n_proto):
        top = jnp.maximum(top, lse_all[q])
    mass = jnp.exp2(lse_all[0] - top)
    for q in range(1, n_proto):
        mass = mass + jnp.exp2(lse_all[q] - top)
    lse = top + jnp.log(mass) * LOG2E
    lse_rows_s = lse[:n_groups]
    gain = jnp.log(weight_tile[...] / student_temp) * LOG2E
    shift_s = lse_rows_s - gain
    shift_t = lse[n_groups:] - gain
    for g in range(n_groups):
        part = slice(g * LANES, (g + 1) * LANES)
        peak_s[part, :] = jnp.broadcast_to(to_column(shift_s[g : g + 1, :]), (LANES, LANES))
        peak_t[part, :] = jnp.broadcast_to(to_column(shift_t[g : g + 1, :]), (LANES, LANES))

    cols_two = 1024
    loss_send[...] = jnp.zeros(loss_send.shape, F32)

    def second_step(j, carry):
        c0 = pl.multiple_of(j * cols_two, cols_two)
        block = pl.ds(c0, cols_two)
        w_block = ws[:, block]
        wt_block = wt[:, block]
        shift = centre[:, block] * SCALE_T
        acc = jnp.zeros((emb, cols_two), F32)
        cross = jnp.zeros((row_chunk, LANES), F32)
        for r in range(n_rows // row_chunk):
            part = slice(r * row_chunk, (r + 1) * row_chunk)
            zs = jnp.dot(rows[part, :emb], w_block, preferred_element_type=F32)
            zt = jnp.dot(rows[part, emb:], wt_block, preferred_element_type=F32)
            a = peak_s[part, :]
            b = peak_t[part, :]
            pieces = []
            for k in range(cols_two // LANES):
                at = slice(k * LANES, (k + 1) * LANES)
                z = zs[:, at]
                target = jnp.exp2(zt[:, at] * SCALE_T - (b + shift[:, at]))
                pieces.append((jnp.exp2(z * SCALE_S - a) - target).astype(BF16))
                cross = cross + target * z
            glog = jnp.concatenate(pieces, axis=1)
            unit_acc[part, :] += lax.dot_general(
                glog, w_block, (((1,), (1,)), ((), ())), preferred_element_type=F32
            )
            acc = acc + jnp.dot(rows_across[:, part], glog, preferred_element_type=F32)
        slab_send[:, :, block] = acc.astype(BF16).reshape(n_dp, slab, cols_two)
        loss_send[...] += jnp.sum(cross.reshape(row_chunk // 8, 8, LANES), axis=0)
        for i in range(1, n_dp):
            t = dp_peer(i)
            push(
                slab_send.at[t, :, block], slab_recv.at[d, :, block], slab_ssem.at[i], slab_rsem.at[d], (t, p)
            ).start()
        return carry

    lax.fori_loop(0, cols // cols_two, second_step, 0)

    unit_send[...] = unit_acc[...].astype(BF16)
    loss_recv[p] = loss_send[...]
    tails = []
    for i in range(1, n_proto):
        q = proto_peer(i)
        tails.append(push(loss_send, loss_recv.at[p], loss_ssem.at[i], loss_rsem.at[p], (d, q)))
        at = pl.ds(pl.multiple_of(q * mask_count, mask_count), mask_count)
        tails.append(push(unit_send.at[at], unit_recv.at[p], unit_ssem.at[i], unit_rsem.at[p], (d, q)))
    for copy in tails:
        copy.start()
    unit_recv[p] = unit_send[own, :]

    for i in range(1, n_proto):
        q = lax.rem(p + n_proto - i, n_proto)
        push(loss_send, loss_recv.at[q], loss_ssem.at[i], loss_rsem.at[q], (d, twin)).wait_recv()
    cross_total = loss_recv[0]
    for q in range(1, n_proto):
        cross_total = cross_total + loss_recv[q]
    group_send[...] = weight_tile[...] * lse_rows_s * LN2 - cross_total
    group_recv[d] = group_send[...]
    group_copies = []
    for i in range(1, n_dp):
        group_copies.append(
            push(group_send, group_recv.at[d], group_ssem.at[i], group_rsem.at[d], (dp_peer(i), p))
        )
    for copy in group_copies:
        copy.start()

    for i in range(1, n_proto):
        q = lax.rem(p + n_proto - i, n_proto)
        push(unit_send.at[own], unit_recv.at[q], unit_ssem.at[i], unit_rsem.at[q], (d, twin)).wait_recv()
    unit_grad = unit_recv[0].astype(F32)
    for q in range(1, n_proto):
        unit_grad = unit_grad + unit_recv[q].astype(F32)
    raw = raw_keep[...]
    inv = inv_keep[:, 0:1]
    dotted = jnp.sum(raw * unit_grad, axis=1, keepdims=True)
    row_grad_out[...] = inv * unit_grad - (inv * inv * inv) * raw * dotted

    for i in range(1, n_dp):
        q = lax.rem(d + n_dp - i, n_dp)
        push(group_send, group_recv.at[q], group_ssem.at[i], group_rsem.at[q], (d, twin)).wait_recv()
    total = group_recv[0]
    for q in range(1, n_dp):
        total = total + group_recv[q]
    total = jnp.sum(jnp.sum(total, axis=0, keepdims=True), axis=1, keepdims=True)
    loss_out[...] = jnp.broadcast_to(total / float(n_rows * n_dp), loss_out.shape)

    for i in range(1, n_dp):
        q = lax.rem(d + n_dp - i, n_dp)
        push(slab_send.at[d], slab_recv.at[q], slab_ssem.at[i], slab_rsem.at[q], (d, twin)).wait_recv()
    slab_recv[d] = slab_send[d]

    def sum_step(j, carry):
        block = pl.ds(pl.multiple_of(j * 1024, 1024), 1024)
        acc = slab_recv[0, :, block].astype(F32)
        for q in range(1, n_dp):
            acc = acc + slab_recv[q, :, block].astype(F32)
        proto_grad_out[:, block] = acc
        return carry

    lax.fori_loop(0, cols // 1024, sum_step, 0)

    for copy in sends + forwards + lse_copies + tails + group_copies:
        copy.wait_send()
    for i in range(1, n_dp):
        t = dp_peer(i)
        push(slab_send.at[t], slab_recv.at[d], slab_ssem.at[i], slab_rsem.at[d], (t, p)).wait_send()


def head(n_dp, n_proto, student_patch, teacher_patch, patch_image, masked_rows, student_proto, teacher_proto, centre):
    mask_count = masked_rows.shape[1]
    emb, cols = student_proto.shape
    n_rows = mask_count * n_proto
    vmem = pl.BlockSpec(memory_space=pltpu.VMEM)
    hbm = pl.BlockSpec(memory_space=pl.ANY)
    dma = pltpu.SemaphoreType.DMA
    slab = emb // n_dp
    n_groups = n_rows // LANES
    return pl.pallas_call(
        functools.partial(head_kernel, n_dp, n_proto),
        out_shape=(
            jax.ShapeDtypeStruct((mask_count, emb), F32),
            jax.ShapeDtypeStruct((slab, cols), F32),
            jax.ShapeDtypeStruct((8, LANES), F32),
        ),
        in_specs=[vmem, vmem, vmem, vmem, hbm, hbm, vmem],
        out_specs=(vmem, vmem, vmem),
        scratch_shapes=[
            pltpu.VMEM((4, emb, 1024), F32),
            pltpu.VMEM((emb, cols), BF16),
            pltpu.VMEM((emb, cols), BF16),
            pltpu.VMEM((n_rows, 2 * emb), BF16),
            pltpu.VMEM((emb, n_rows), BF16),
            pltpu.VMEM((mask_count, emb), F32),
            pltpu.VMEM((mask_count, LANES), F32),
            pltpu.VMEM((n_proto, 8, LANES), F32),
            pltpu.VMEM((n_rows, LANES), F32),
            pltpu.VMEM((n_rows, LANES), F32),
            pltpu.VMEM((n_rows, LANES), F32),
            pltpu.VMEM((n_rows, LANES), F32),
            pltpu.VMEM((n_groups, LANES), F32),
            pltpu.VMEM((2 * n_groups, LANES), F32),
            pltpu.VMEM((n_proto, 2 * n_groups, LANES), F32),
            pltpu.VMEM((n_rows, emb), F32),
            pltpu.VMEM((n_rows, emb), BF16),
            pltpu.VMEM((n_proto, mask_count, emb), BF16),
            pltpu.VMEM((n_dp, slab, cols), BF16),
            pltpu.VMEM((n_dp, slab, cols), BF16),
            pltpu.VMEM((8, LANES), F32),
            pltpu.VMEM((n_proto, 8, LANES), F32),
            pltpu.VMEM((8, LANES), F32),
            pltpu.VMEM((n_dp, 8, LANES), F32),
            dma((4,)),
        ]
        + [dma((n_proto,))] * 8
        + [dma((n_dp,))] * 2
        + [dma((n_proto,))] * 2
        + [dma((n_dp,))] * 2,
        compiler_params=pltpu.CompilerParams(
            collective_id=0, has_side_effects=True, vmem_limit_bytes=60 * 1024 * 1024
        ),
        name="head",
    )(student_patch, teacher_patch, patch_image, masked_rows, student_proto, teacher_proto, centre)


def local(
    student_patch,
    teacher_patch,
    patch_image,
    masked_rows,
    student_proto,
    teacher_proto,
    first_moment,
    second_moment,
    centre,
):
    n_proto = lax.axis_size("proto")
    n_dp = lax.axis_size("dp")
    row_grad, proto_grad, loss = head(
        n_dp,
        n_proto,
        student_patch[0],
        teacher_patch[0],
        patch_image,
        masked_rows,
        student_proto,
        teacher_proto,
        centre[None, :],
    )
    slab_rows = first_moment.shape[0]
    slab_start = lax.axis_index("dp") * slab_rows
    own_student = lax.dynamic_slice_in_dim(student_proto, slab_start, slab_rows, 0)
    own_teacher = lax.dynamic_slice_in_dim(teacher_proto, slab_start, slab_rows, 0)
    new_first = beta_one * first_moment + (1.0 - beta_one) * proto_grad
    new_second = beta_two * second_moment + (1.0 - beta_two) * proto_grad * proto_grad
    step_size = new_first / fix_one / (jnp.sqrt(new_second / fix_two) + 1e-08)
    new_student = own_student - learn_rate * (step_size + decay_rate * own_student)
    new_teacher = teacher_keep * own_teacher + (1.0 - teacher_keep) * new_student
    return (row_grad[None], new_student, new_first, new_second, new_teacher, loss[0, 0])


def solution(mesh):
    in_specs = (
        P("dp", "proto", None),
        P("dp", "proto", None),
        P("dp", "proto"),
        P("dp", "proto"),
        P(None, "proto"),
        P(None, "proto"),
        P("dp", "proto"),
        P("dp", "proto"),
        P("proto"),
    )
    out_specs = (
        P("dp", "proto", None),
        P("dp", "proto"),
        P("dp", "proto"),
        P("dp", "proto"),
        P("dp", "proto"),
        P(),
    )
    return jax.shard_map(local, mesh=mesh, in_specs=in_specs, out_specs=out_specs, check_vma=False)
```

```python
import functools
import math

import jax
import jax.numpy as jnp
from jax import lax
from jax.experimental import pallas as pl
from jax.experimental.pallas import tpu as pltpu
from jax.sharding import PartitionSpec as P

PATCH_IMG = 256
IMG_GROUP = 8

student_temp = 0.1
teacher_temp = 0.07
beta_one = 0.9
beta_two = 0.999
fix_one = 0.9999734386011124
fix_two = 0.09520785288629038
learn_rate = 0.002
decay_rate = 0.04
teacher_keep = 0.994

F32 = jnp.float32
BF16 = jnp.bfloat16
MESH = pl.DeviceIdType.MESH
LOG2E = math.log2(math.e)
LN2 = math.log(2.0)
SCALE_S = LOG2E / student_temp
SCALE_T = LOG2E / teacher_temp
LOWEST = -3.0e38
LANES = 128
HALVES = 2


def iota(shape, axis):
    return lax.broadcasted_iota(jnp.int32, shape, axis)


def eye(n):
    return iota((n, n), 0) == iota((n, n), 1)


def to_column(row):
    n = row.shape[1]
    return jnp.sum(jnp.where(eye(n), jnp.broadcast_to(row, (n, n)), 0.0), axis=1, keepdims=True)


def to_row(column):
    n = column.shape[0]
    return jnp.sum(jnp.where(eye(n), jnp.broadcast_to(column, (n, n)), 0.0), axis=0, keepdims=True)


def head_kernel(
    n_dp,
    n_proto,
    student_patch,
    teacher_patch,
    patch_image,
    masked_rows,
    student_hbm,
    teacher_hbm,
    centre,
    row_grad_out,
    proto_grad_out,
    loss_out,
    stage,
    ws,
    wt,
    rows,
    rows_across,
    raw_keep,
    inv_keep,
    ids,
    peak_s,
    sum_s,
    peak_t,
    sum_t,
    shift_s,
    shift_t,
    weight_tile,
    lse_tile,
    lse_send,
    lse_all,
    unit_acc,
    unit_send,
    unit_recv,
    slab_send,
    slab_recv,
    both,
    half_send,
    half_recv,
    loss_acc,
    loss_send,
    loss_recv,
    group_recv,
    stage_sem,
    row_ssem,
    hand_ssem,
    row_rsem,
    id_ssem,
    id_rsem,
    lse_ssem,
    lse_rsem,
    unit_ssem,
    unit_rsem,
    slab_ssem,
    slab_rsem,
    half_ssem,
    half_rsem,
    loss_ssem,
    loss_rsem,
    group_ssem,
    group_rsem,
):
    n_y = n_dp // HALVES
    n_plane = HALVES * n_proto
    n_z = 2 * HALVES
    n_x = n_plane // (2 * n_z)
    d = lax.axis_index("dp")
    p = lax.axis_index("proto")
    y = d // HALVES
    zh = lax.rem(d, HALVES)
    me = zh * n_proto + p
    z = me // (2 * n_x)
    x = lax.rem(me // 2, n_x)
    core = lax.rem(p, 2)
    twin = me + 1 - 2 * core
    mask_count = masked_rows.shape[1]
    patch_count = patch_image.shape[1]
    emb, cols = ws.shape
    n_rows = rows.shape[0]
    chunk = n_rows // n_z
    slab = emb // n_y
    part_rows = slab // HALVES
    load_cols = stage.shape[2]
    row_chunk = 256
    tiles = chunk // LANES
    group_tiles = n_rows // LANES // HALVES
    first_col = zh * cols

    def place(q):
        return (HALVES * y + q // n_proto, lax.rem(q, n_proto))

    def ring(i):
        return lax.rem(me + i, n_plane)

    def back(i):
        return lax.rem(me + n_plane - i, n_plane)

    def push(src, dst, ssem, rsem, target):
        return pltpu.make_async_remote_copy(
            src_ref=src, dst_ref=dst, send_sem=ssem, recv_sem=rsem, device_id=target, device_id_type=MESH
        )

    def each(count, body):
        def step(i, carry):
            body(i)
            return carry

        lax.fori_loop(1, count, step, 0)

    barrier = pltpu.get_barrier_semaphore()

    def y_peer(i):
        return (HALVES * lax.rem(y + i, n_y) + zh, p)

    each(n_plane, lambda i: pl.semaphore_signal(barrier, inc=1, device_id=place(ring(i)), device_id_type=MESH))
    each(n_y, lambda i: pl.semaphore_signal(barrier, inc=1, device_id=y_peer(i), device_id_type=MESH))

    n_load = cols // load_cols

    def load(hbm, j, slot):
        c0 = pl.multiple_of(first_col + j * load_cols, load_cols)
        return pltpu.make_async_copy(hbm.at[:, pl.ds(c0, load_cols)], stage.at[slot], stage_sem.at[slot])

    load(student_hbm, 0, 0).start()
    load(teacher_hbm, 0, 1).start()
    load(student_hbm, 1, 2).start()
    load(teacher_hbm, 1, 3).start()

    picked = to_column(masked_rows[...].astype(F32))
    one_hot = iota((mask_count, patch_count), 1).astype(F32) == picked
    one_hot_f = jnp.where(one_hot, 1.0, 0.0)
    one_hot_b = one_hot_f.astype(BF16)
    raw_s = jnp.dot(one_hot_b, student_patch[...], preferred_element_type=F32)
    raw_t = jnp.dot(one_hot_b, teacher_patch[...], preferred_element_type=F32)
    inv_s = lax.rsqrt(jnp.sum(raw_s * raw_s, axis=1, keepdims=True) + 1e-06)
    inv_t = lax.rsqrt(jnp.sum(raw_t * raw_t, axis=1, keepdims=True) + 1e-06)

    def span(q):
        return pl.ds(pl.multiple_of(q * mask_count, mask_count), mask_count)

    rows[span(me), :emb] = (raw_s * inv_s).astype(BF16)
    rows[span(me), emb:] = (raw_t * inv_t).astype(BF16)
    raw_keep[...] = raw_s
    inv_keep[...] = jnp.broadcast_to(inv_s, inv_keep.shape)
    own_ids = to_row(jnp.sum(one_hot_f * patch_image[...].astype(F32), axis=1, keepdims=True))
    ids[me] = jnp.concatenate([own_ids, own_ids], axis=1)

    pl.semaphore_wait(barrier, n_plane + n_y - 2)

    def at(z_at, x_at):
        return (lax.rem(z_at, n_z) * n_x + lax.rem(x_at, n_x)) * 2 + core

    def row_copy(dz, dx):
        i = dz * n_x + dx
        block = rows.at[span(me)]
        return push(block, block, row_ssem.at[i], row_rsem.at[me], place(at(z + dz, x + dx)))

    def row_arrival(q):
        block = rows.at[span(q)]
        return push(block, block, row_ssem.at[0], row_rsem.at[q], place(twin))

    def hand_on(dz, dx):
        q = at(z + n_z - dz, x + n_x - dx)
        block = rows.at[span(q)]
        return push(block, block, hand_ssem.at[dz * n_x + dx], row_rsem.at[q], place(twin))

    hand_on(0, 0).start()
    order = [0, 1, 3, 2]
    for dz in order:
        for dx in order:
            if dz or dx:
                row_copy(dz, dx).start()

    def id_copy(i):
        return push(ids.at[me], ids.at[me], id_ssem.at[i], id_rsem.at[me], place(ring(i)))

    each(n_plane, lambda i: id_copy(i).start())

    def cast_step(j, carry):
        c0 = pl.multiple_of(j * load_cols, load_cols)
        odd = lax.rem(j, 2) * 2
        load(student_hbm, j, odd).wait()
        ws[:, pl.ds(c0, load_cols)] = stage[odd].astype(BF16)

        @pl.when(j + 2 < n_load)
        def _():
            load(student_hbm, j + 2, odd).start()

        load(teacher_hbm, j, odd + 1).wait()
        wt[:, pl.ds(c0, load_cols)] = stage[odd + 1].astype(BF16)

        @pl.when(j + 2 < n_load)
        def _():
            load(teacher_hbm, j + 2, odd + 1).start()

        return carry

    lax.fori_loop(0, n_load, cast_step, 0)

    def take_direct(dz, skip_own=False):
        for dx in order:
            if not (skip_own and dx == 0):
                row_arrival(at(z + n_z - dz, x + n_x - dx)).wait_recv()
                hand_on(dz, dx).start()

    def take_handed(dz):
        for dx in order:
            row_arrival(at(z + n_z - dz, x + n_x - dx) + 1 - 2 * core).wait_recv()

    take_direct(0, skip_own=True)
    take_handed(0)

    cols_one = 512
    n_one = cols // cols_one

    def lse_copy(k_at, i):
        return push(
            lse_send.at[k_at], lse_all.at[k_at, me], lse_ssem.at[k_at, i], lse_rsem.at[k_at, me], place(ring(i))
        )

    def chunk_step(k, carry):
        dz = k + (k // 2) * (1 - 2 * lax.rem(k, 2))
        after = k + 1
        dz_after = after + (after // 2) * (1 - 2 * lax.rem(after, 2))
        z_at = lax.rem(z + n_z - dz, n_z)
        for peak, total in ((peak_s, sum_s), (peak_t, sum_t)):
            peak[...] = jnp.full(peak.shape, LOWEST, F32)
            total[...] = jnp.zeros(total.shape, F32)

        def first_step(j, inner):
            c0 = pl.multiple_of(j * cols_one, cols_one)
            for r in range(chunk // row_chunk):
                part = slice(r * row_chunk, (r + 1) * row_chunk)
                here = pl.ds(pl.multiple_of(z_at * chunk + r * row_chunk, row_chunk), row_chunk)
                for e0, w, peak, total, scale, shift in (
                    (0, ws, peak_s, sum_s, SCALE_S, False),
                    (emb, wt, peak_t, sum_t, SCALE_T, True),
                ):
                    logit = jnp.dot(
                        rows[here, e0 : e0 + emb], w[:, pl.ds(c0, cols_one)], preferred_element_type=F32
                    )
                    if shift:
                        logit = logit - centre[:, pl.ds(pl.multiple_of(first_col + c0, cols_one), cols_one)]
                    pieces = [logit[:, n * LANES : (n + 1) * LANES] for n in range(cols_one // LANES)]
                    before = peak[part, :]
                    now = before
                    for piece in pieces:
                        now = jnp.maximum(now, piece)
                    acc = total[part, :] * jnp.exp2((before - now) * scale)
                    for piece in pieces:
                        acc = acc + jnp.exp2((piece - now) * scale)
                    total[part, :] = acc
                    peak[part, :] = now
            return inner

        lax.fori_loop(0, n_one // 2, first_step, 0)

        @pl.when(after < n_z)
        def _():
            take_direct(dz_after)

        lax.fori_loop(n_one // 2, n_one, first_step, 0)

        for n, (peak, total, scale) in enumerate(((peak_s, sum_s, SCALE_S), (peak_t, sum_t, SCALE_T))):
            for g in range(tiles):
                part = slice(g * LANES, (g + 1) * LANES)
                lanes_peak = peak[part, :]
                top = jnp.max(lanes_peak, axis=1, keepdims=True)
                mass = jnp.sum(total[part, :] * jnp.exp2((lanes_peak - top) * scale), axis=1, keepdims=True)
                r = n * tiles + g
                lse_tile[r : r + 1, :] = to_row(top * scale + jnp.log(mass) * LOG2E)
        lse_send[z_at] = lse_tile[...]
        lse_all[z_at, me] = lse_tile[...]
        each(n_plane, lambda i: lse_copy(z_at, i).start())

        @pl.when(after < n_z)
        def _():
            take_handed(dz_after)

        return carry

    lax.fori_loop(0, n_z, chunk_step, 0)

    rows_across[...] = rows[:, :emb].T
    unit_acc[...] = jnp.zeros(unit_acc.shape, F32)

    each(n_plane, lambda i: push(
        ids.at[back(i)], ids.at[back(i)], id_ssem.at[i], id_rsem.at[back(i)], place(twin)
    ).wait_recv())
    lane = iota((1, LANES), 1)
    row_ratio = float(mask_count * PATCH_IMG // patch_count)
    for half in range(HALVES):
        id_rows = []
        for g in range(half * group_tiles, (half + 1) * group_tiles):
            id_rows.append(jnp.where(lane < mask_count, ids[2 * g], ids[2 * g + 1]))
        id_tile = jnp.concatenate(id_rows, axis=0)
        weight = jnp.zeros_like(id_tile)
        for label in range(IMG_GROUP):
            hits = jnp.where(id_tile == float(label), 1.0, 0.0)
            count = jnp.sum(jnp.sum(hits, axis=0, keepdims=True), axis=1, keepdims=True)
            weight = weight + hits * (row_ratio / jnp.maximum(count, 1.0))
        weight_tile[half * group_tiles : (half + 1) * group_tiles, :] = weight

    loss_acc[...] = jnp.zeros(loss_acc.shape, F32)
    for z_at in range(n_z):
        each(n_plane, lambda i: push(
            lse_send.at[z_at], lse_all.at[z_at, back(i)], lse_ssem.at[z_at, i], lse_rsem.at[z_at, back(i)], place(twin)
        ).wait_recv())
        top = lse_all[z_at, 0]
        for q in range(1, n_plane):
            top = jnp.maximum(top, lse_all[z_at, q])
        mass = jnp.exp2(lse_all[z_at, 0] - top)
        for q in range(1, n_plane):
            mass = mass + jnp.exp2(lse_all[z_at, q] - top)
        lse = top + jnp.log(mass) * LOG2E
        weight = weight_tile[z_at * tiles : (z_at + 1) * tiles, :]
        gain = jnp.log(weight / student_temp) * LOG2E
        lse_tile[:tiles, :] = lse[:tiles] - gain
        lse_tile[tiles:, :] = lse[tiles:] - gain
        loss_acc[:tiles, :] += weight * lse[:tiles] * LN2
        for g in range(tiles):
            part = slice(z_at * chunk + g * LANES, z_at * chunk + (g + 1) * LANES)
            shift_s[part, :] = jnp.broadcast_to(to_column(lse_tile[g : g + 1, :]), (LANES, LANES))
            shift_t[part, :] = jnp.broadcast_to(to_column(lse_tile[tiles + g : tiles + g + 1, :]), (LANES, LANES))

    cols_two = 512
    rows_two = 512
    n_two = cols // cols_two
    lag = 2
    loss_send[...] = jnp.zeros(loss_send.shape, F32)
    partner = (HALVES * y + 1 - zh, p)

    def block_at(j):
        return pl.ds(pl.multiple_of(j * cols_two, cols_two), cols_two)

    def slab_copy(j, i):
        to = lax.rem(y + i, n_y)
        return push(
            slab_send.at[to, :, block_at(j)],
            slab_recv.at[y, :, block_at(j)],
            slab_ssem.at[i, j],
            slab_rsem.at[y, j],
            y_peer(i),
        )

    def slab_arrival(j, i):
        origin = lax.rem(y + n_y - i, n_y)
        return push(
            slab_send.at[y, :, block_at(j)],
            slab_recv.at[origin, :, block_at(j)],
            slab_ssem.at[i, j],
            slab_rsem.at[origin, j],
            partner,
        )

    def half_copy(j):
        return push(half_send.at[:, block_at(j)], half_recv.at[:, block_at(j)], half_ssem.at[j], half_rsem.at[j], partner)

    def unit_copy(i_sem, q):
        return push(unit_send.at[span(q)], unit_recv.at[me], unit_ssem.at[i_sem], unit_rsem.at[me], place(q))

    def settle(j):
        block = block_at(j)
        for i in range(1, n_y):
            slab_arrival(j, i).wait_recv()
        acc = slab_send[y, :, block].astype(F32)
        for i in range(1, n_y):
            acc = acc + slab_recv[lax.rem(y + n_y - i, n_y), :, block].astype(F32)
        both[...] = acc.reshape(HALVES, part_rows, cols_two)
        proto_grad_out[:, pl.ds(pl.multiple_of(first_col + j * cols_two, cols_two), cols_two)] = both[zh]
        half_send[:, block] = both[1 - zh].astype(BF16)
        half_copy(j).start()

    def second_block(j, last):
        block = block_at(j)
        w_block = ws[:, block]
        wt_block = wt[:, block]
        shift = centre[:, pl.ds(pl.multiple_of(first_col + j * cols_two, cols_two), cols_two)] * SCALE_T
        acc = jnp.zeros((emb, cols_two), F32)
        cross = jnp.zeros((rows_two, LANES), F32)
        n_parts = n_rows // rows_two
        owners = rows_two // mask_count
        for r in range(n_parts):
            index = lax.rem(r + 1 + me // owners, n_parts) if last else r
            part = pl.ds(pl.multiple_of(index * rows_two, rows_two), rows_two)
            zs = jnp.dot(rows[part, :emb], w_block, preferred_element_type=F32)
            zt = jnp.dot(rows[part, emb:], wt_block, preferred_element_type=F32)
            a = shift_s[part, :]
            b = shift_t[part, :]
            pieces = []
            for n in range(cols_two // LANES):
                cut = slice(n * LANES, (n + 1) * LANES)
                logit = zs[:, cut]
                target = jnp.exp2(zt[:, cut] * SCALE_T - (b + shift[:, cut]))
                pieces.append((jnp.exp2(logit * SCALE_S - a) - target).astype(BF16))
                cross = cross + target * logit
            glog = jnp.concatenate(pieces, axis=1)
            product = lax.dot_general(glog, w_block, (((1,), (1,)), ((), ())), preferred_element_type=F32)
            acc = acc + jnp.dot(rows_across[:, part], glog, preferred_element_type=F32)
            if last:
                unit_send[part, :] = (unit_acc[part, :] + product).astype(BF16)
                for n in range(owners):
                    q = index * owners + n
                    if r < n_parts - 1:
                        unit_copy(r * owners + n, q).start()
                    else:

                        @pl.when(q != me)
                        def _():
                            unit_copy(r * owners + n, q).start()
            else:
                unit_acc[part, :] += product
        slab_send[:, :, block] = acc.astype(BF16).reshape(n_y, slab, cols_two)
        loss_send[...] += jnp.sum(jnp.sum(cross.reshape(rows_two // 8, 8, LANES), axis=0), axis=0, keepdims=True)
        for i in range(1, n_y):
            slab_copy(j, i).start()

    def second_step(j, carry):
        second_block(j, False)

        @pl.when(j >= lag)
        def _():
            settle(j - lag)

        return carry

    lax.fori_loop(0, n_two - 1, second_step, 0)
    second_block(n_two - 1, True)

    loss_recv[me] = loss_send[...]

    def loss_copy(i):
        return push(loss_send, loss_recv.at[me], loss_ssem.at[i], loss_rsem.at[me], place(ring(i)))

    each(n_plane, lambda i: loss_copy(i).start())
    unit_recv[me] = unit_send[span(me), :]
    settle(n_two - 1 - lag)
    settle(n_two - lag)

    each(n_plane, lambda i: push(
        loss_send, loss_recv.at[back(i)], loss_ssem.at[i], loss_rsem.at[back(i)], place(twin)
    ).wait_recv())
    cross_total = loss_recv[0]
    for q in range(1, n_plane):
        cross_total = cross_total + loss_recv[q]
    group_recv[y] = jnp.sum(loss_acc[...], axis=0, keepdims=True) - cross_total

    def group_copy(i):
        return push(group_recv.at[y], group_recv.at[y], group_ssem.at[i], group_rsem.at[y], y_peer(i))

    for i in range(1, n_y):
        group_copy(i).start()

    settle(n_two - 1)

    each(n_plane, lambda i: push(
        unit_send.at[span(me)], unit_recv.at[back(i)], unit_ssem.at[i], unit_rsem.at[back(i)], place(twin)
    ).wait_recv())
    unit_grad = unit_recv[0].astype(F32)
    for q in range(1, n_plane):
        unit_grad = unit_grad + unit_recv[q].astype(F32)
    raw = raw_keep[...]
    inv = inv_keep[:, 0:1]
    dotted = jnp.sum(raw * unit_grad, axis=1, keepdims=True)
    row_grad_out[...] = inv * unit_grad - (inv * inv * inv) * raw * dotted

    for i in range(1, n_y):
        q = lax.rem(y + n_y - i, n_y)
        push(group_recv.at[y], group_recv.at[q], group_ssem.at[i], group_rsem.at[q], partner).wait_recv()
    total = group_recv[0]
    for q in range(1, n_y):
        total = total + group_recv[q]
    loss_out[0, 0] = jnp.sum(total) * (1.0 / float(n_rows * n_y))

    other_col = (1 - zh) * cols
    for j in range(n_two):
        half_copy(j).wait_recv()
        to = pl.ds(pl.multiple_of(other_col + j * cols_two, cols_two), cols_two)
        proto_grad_out[:, to] = half_recv[:, j * cols_two : (j + 1) * cols_two].astype(F32)

    for dz in order:
        for dx in order:
            if dz or dx:
                row_copy(dz, dx).wait_send()
            hand_on(dz, dx).wait_send()

    def sent(i):
        id_copy(i).wait_send()
        loss_copy(i).wait_send()
        for z_at in range(n_z):
            lse_copy(z_at, i).wait_send()

    each(n_plane, sent)
    owners = rows_two // mask_count
    n_parts = n_rows // rows_two
    for r in range(n_parts):
        for n in range(owners):
            q = lax.rem(r + 1 + me // owners, n_parts) * owners + n
            if r < n_parts - 1:
                unit_copy(r * owners + n, q).wait_send()
            else:

                @pl.when(q != me)
                def _():
                    unit_copy(r * owners + n, q).wait_send()

    for j in range(n_two):
        half_copy(j).wait_send()
        for i in range(1, n_y):
            slab_copy(j, i).wait_send()
    for i in range(1, n_y):
        group_copy(i).wait_send()


def head(n_dp, n_proto, student_patch, teacher_patch, patch_image, masked_rows, student_proto, teacher_proto, centre):
    mask_count = masked_rows.shape[1]
    emb, all_cols = student_proto.shape
    cols = all_cols // HALVES
    n_plane = n_proto * HALVES
    n_y = n_dp // HALVES
    n_z = 2 * HALVES
    n_rows = mask_count * n_plane
    chunk = n_rows // n_z
    vmem = pl.BlockSpec(memory_space=pltpu.VMEM)
    hbm = pl.BlockSpec(memory_space=pl.ANY)
    dma = pltpu.SemaphoreType.DMA
    slab = emb // n_y
    blocks = cols // 512
    return pl.pallas_call(
        functools.partial(head_kernel, n_dp, n_proto),
        out_shape=(
            jax.ShapeDtypeStruct((mask_count, emb), F32),
            jax.ShapeDtypeStruct((slab // HALVES, all_cols), F32),
            jax.ShapeDtypeStruct((1, 1), F32),
        ),
        in_specs=[vmem, vmem, vmem, vmem, hbm, hbm, vmem],
        out_specs=(vmem, vmem, pl.BlockSpec(memory_space=pltpu.SMEM)),
        scratch_shapes=[
            pltpu.VMEM((4, emb, 1024), F32),
            pltpu.VMEM((emb, cols), BF16),
            pltpu.VMEM((emb, cols), BF16),
            pltpu.VMEM((n_rows, 2 * emb), BF16),
            pltpu.VMEM((emb, n_rows), BF16),
            pltpu.VMEM((mask_count, emb), F32),
            pltpu.VMEM((mask_count, LANES), F32),
            pltpu.VMEM((n_plane, 1, LANES), F32),
            pltpu.VMEM((chunk, LANES), F32),
            pltpu.VMEM((chunk, LANES), F32),
            pltpu.VMEM((chunk, LANES), F32),
            pltpu.VMEM((chunk, LANES), F32),
            pltpu.VMEM((n_rows, LANES), F32),
            pltpu.VMEM((n_rows, LANES), F32),
            pltpu.VMEM((n_rows // LANES, LANES), F32),
            pltpu.VMEM((8, LANES), F32),
            pltpu.VMEM((n_z, 8, LANES), F32),
            pltpu.VMEM((n_z, n_plane, 8, LANES), F32),
            pltpu.VMEM((n_rows, emb), F32),
            pltpu.VMEM((n_rows, emb), BF16),
            pltpu.VMEM((n_plane, mask_count, emb), BF16),
            pltpu.VMEM((n_y, slab, cols), BF16),
            pltpu.VMEM((n_y, slab, cols), BF16),
            pltpu.VMEM((HALVES, slab // HALVES, 512), F32),
            pltpu.VMEM((slab // HALVES, cols), BF16),
            pltpu.VMEM((slab // HALVES, cols), BF16),
            pltpu.VMEM((8, LANES), F32),
            pltpu.VMEM((1, LANES), F32),
            pltpu.VMEM((n_plane, 1, LANES), F32),
            pltpu.VMEM((n_y, 1, LANES), F32),
            dma((4,)),
            dma((n_plane // 2,)),
            dma((n_plane // 2,)),
            dma((n_plane,)),
            dma((n_plane,)),
            dma((n_plane,)),
            dma((n_z, n_plane)),
            dma((n_z, n_plane)),
            dma((n_plane,)),
            dma((n_plane,)),
            dma((n_y, blocks)),
            dma((n_y, blocks)),
            dma((blocks,)),
            dma((blocks,)),
            dma((n_plane,)),
            dma((n_plane,)),
            dma((n_y,)),
            dma((n_y,)),
        ],
        compiler_params=pltpu.CompilerParams(
            collective_id=0, has_side_effects=True, vmem_limit_bytes=56 * 1024 * 1024
        ),
        name="head",
    )(student_patch, teacher_patch, patch_image, masked_rows, student_proto, teacher_proto, centre)


def local(
    student_patch,
    teacher_patch,
    patch_image,
    masked_rows,
    student_proto,
    teacher_proto,
    first_moment,
    second_moment,
    centre,
):
    n_proto = lax.axis_size("proto")
    n_dp = lax.axis_size("dp")
    row_grad, proto_grad, loss = head(
        n_dp,
        n_proto,
        student_patch[0],
        teacher_patch[0],
        patch_image,
        masked_rows,
        student_proto,
        teacher_proto,
        centre[None, :],
    )
    slab_rows = first_moment.shape[0]
    slab_start = lax.axis_index("dp") * slab_rows
    own_student = lax.dynamic_slice_in_dim(student_proto, slab_start, slab_rows, 0)
    own_teacher = lax.dynamic_slice_in_dim(teacher_proto, slab_start, slab_rows, 0)
    new_first = beta_one * first_moment + (1.0 - beta_one) * proto_grad
    new_second = beta_two * second_moment + (1.0 - beta_two) * proto_grad * proto_grad
    step_size = new_first / fix_one / (jnp.sqrt(new_second / fix_two) + 1e-08)
    new_student = own_student - learn_rate * (step_size + decay_rate * own_student)
    new_teacher = teacher_keep * own_teacher + (1.0 - teacher_keep) * new_student
    return (row_grad[None], new_student, new_first, new_second, new_teacher, loss[0, 0])


def solution(mesh):
    in_specs = (
        P("dp", "proto", None),
        P("dp", "proto", None),
        P("dp", "proto"),
        P("dp", "proto"),
        P(None, "proto"),
        P(None, "proto"),
        P("dp", "proto"),
        P("dp", "proto"),
        P("proto"),
    )
    out_specs = (
        P("dp", "proto", None),
        P("dp", "proto"),
        P("dp", "proto"),
        P("dp", "proto"),
        P("dp", "proto"),
        P(),
    )
    return jax.shard_map(local, mesh=mesh, in_specs=in_specs, out_specs=out_specs, check_vma=False)
```

```python
import functools
import math

import jax
import jax.numpy as jnp
from jax import lax
from jax.experimental import pallas as pl
from jax.experimental.pallas import tpu as pltpu
from jax.sharding import PartitionSpec as P

PATCH_IMG = 256
IMG_GROUP = 8

student_temp = 0.1
teacher_temp = 0.07
beta_one = 0.9
beta_two = 0.999
fix_one = 0.9999734386011124
fix_two = 0.09520785288629038
learn_rate = 0.002
decay_rate = 0.04
teacher_keep = 0.994

F32 = jnp.float32
BF16 = jnp.bfloat16
MESH = pl.DeviceIdType.MESH
LOG2E = math.log2(math.e)
LN2 = math.log(2.0)
SCALE_S = LOG2E / student_temp
SCALE_T = LOG2E / teacher_temp
LOWEST = -3.0e38
LANES = 128
HALVES = 2


def iota(shape, axis):
    return lax.broadcasted_iota(jnp.int32, shape, axis)


def eye(n):
    return iota((n, n), 0) == iota((n, n), 1)


def to_column(row):
    n = row.shape[1]
    return jnp.sum(jnp.where(eye(n), jnp.broadcast_to(row, (n, n)), 0.0), axis=1, keepdims=True)


def to_row(column):
    n = column.shape[0]
    return jnp.sum(jnp.where(eye(n), jnp.broadcast_to(column, (n, n)), 0.0), axis=0, keepdims=True)


def head_kernel(
    n_dp,
    n_proto,
    student_patch_hbm,
    teacher_patch_hbm,
    patch_image_hbm,
    masked_rows_hbm,
    student_hbm,
    teacher_hbm,
    centre_hbm,
    row_grad_out,
    proto_grad_out,
    loss_out,
    student_patch,
    teacher_patch,
    patch_image,
    masked_rows,
    centre,
    stage,
    ws,
    wt,
    rows,
    rows_across,
    raw_keep,
    inv_keep,
    ids,
    peak_s,
    sum_s,
    peak_t,
    sum_t,
    shift_s,
    shift_t,
    weight_tile,
    lse_tile,
    lse_send,
    lse_all,
    unit_acc,
    unit_send,
    unit_recv,
    twin_recv,
    slab_send,
    slab_recv,
    both,
    half_send,
    half_recv,
    loss_acc,
    loss_send,
    loss_recv,
    group_recv,
    input_sem,
    stage_sem,
    row_ssem,
    hand_ssem,
    row_rsem,
    id_ssem,
    id_rsem,
    lse_ssem,
    lse_rsem,
    unit_ssem,
    unit_rsem,
    twin_ssem,
    twin_rsem,
    slab_ssem,
    slab_rsem,
    half_ssem,
    half_rsem,
    loss_ssem,
    loss_rsem,
    group_ssem,
    group_rsem,
):
    n_y = n_dp // HALVES
    n_plane = HALVES * n_proto
    n_z = 2 * HALVES
    n_x = n_plane // (2 * n_z)
    d = lax.axis_index("dp")
    p = lax.axis_index("proto")
    y = d // HALVES
    zh = lax.rem(d, HALVES)
    me = zh * n_proto + p
    z = me // (2 * n_x)
    x = lax.rem(me // 2, n_x)
    core = lax.rem(p, 2)
    twin = me + 1 - 2 * core
    mask_count = masked_rows.shape[1]
    patch_count = patch_image.shape[1]
    emb, cols = ws.shape
    n_rows = rows.shape[0]
    chunk = n_rows // n_z
    slab = emb // n_y
    part_rows = slab // HALVES
    load_cols = stage.shape[2]
    row_chunk = 256
    tiles = chunk // LANES
    group_tiles = n_rows // LANES // HALVES
    first_col = zh * cols

    def place(q):
        return (HALVES * y + q // n_proto, lax.rem(q, n_proto))

    def ring(i):
        return lax.rem(me + i, n_plane)

    def back(i):
        return lax.rem(me + n_plane - i, n_plane)

    def push(src, dst, ssem, rsem, target):
        return pltpu.make_async_remote_copy(
            src_ref=src, dst_ref=dst, send_sem=ssem, recv_sem=rsem, device_id=target, device_id_type=MESH
        )

    def each(count, body):
        def step(i, carry):
            body(i)
            return carry

        lax.fori_loop(1, count, step, 0)

    inputs = []
    for n, (src, dst) in enumerate(
        (
            (masked_rows_hbm, masked_rows),
            (student_patch_hbm, student_patch),
            (teacher_patch_hbm, teacher_patch),
            (patch_image_hbm, patch_image),
            (centre_hbm, centre),
        )
    ):
        inputs.append(pltpu.make_async_copy(src, dst, input_sem.at[n]))
        inputs[-1].start()

    barrier = pltpu.get_barrier_semaphore()

    def y_peer(i):
        return (HALVES * lax.rem(y + i, n_y) + zh, p)

    each(n_plane, lambda i: pl.semaphore_signal(barrier, inc=1, device_id=place(ring(i)), device_id_type=MESH))
    each(n_y, lambda i: pl.semaphore_signal(barrier, inc=1, device_id=y_peer(i), device_id_type=MESH))

    n_load = cols // load_cols

    def load(hbm, j, slot):
        c0 = pl.multiple_of(first_col + j * load_cols, load_cols)
        return pltpu.make_async_copy(hbm.at[:, pl.ds(c0, load_cols)], stage.at[slot], stage_sem.at[slot])

    load(student_hbm, 0, 0).start()
    load(teacher_hbm, 0, 1).start()
    load(student_hbm, 1, 2).start()
    load(teacher_hbm, 1, 3).start()

    for copy in inputs:
        copy.wait()
    picked = to_column(masked_rows[...].astype(F32))
    one_hot = iota((mask_count, patch_count), 1).astype(F32) == picked
    one_hot_f = jnp.where(one_hot, 1.0, 0.0)
    one_hot_b = one_hot_f.astype(BF16)
    raw_s = jnp.dot(one_hot_b, student_patch[...], preferred_element_type=F32)
    raw_t = jnp.dot(one_hot_b, teacher_patch[...], preferred_element_type=F32)
    inv_s = lax.rsqrt(jnp.sum(raw_s * raw_s, axis=1, keepdims=True) + 1e-06)
    inv_t = lax.rsqrt(jnp.sum(raw_t * raw_t, axis=1, keepdims=True) + 1e-06)

    def span(q):
        return pl.ds(pl.multiple_of(q * mask_count, mask_count), mask_count)

    rows[span(me), :emb] = (raw_s * inv_s).astype(BF16)
    rows[span(me), emb:] = (raw_t * inv_t).astype(BF16)
    raw_keep[...] = raw_s
    inv_keep[...] = jnp.broadcast_to(inv_s, inv_keep.shape)
    own_ids = to_row(jnp.sum(one_hot_f * patch_image[...].astype(F32), axis=1, keepdims=True))
    ids[me] = jnp.concatenate([own_ids, own_ids], axis=1)

    pl.semaphore_wait(barrier, n_plane + n_y - 2)

    def at(z_at, x_at):
        return (lax.rem(z_at, n_z) * n_x + lax.rem(x_at, n_x)) * 2 + core

    def row_copy(dz, dx):
        i = dz * n_x + dx
        block = rows.at[span(me)]
        return push(block, block, row_ssem.at[i], row_rsem.at[me], place(at(z + dz, x + dx)))

    def row_arrival(q):
        block = rows.at[span(q)]
        return push(block, block, row_ssem.at[0], row_rsem.at[q], place(twin))

    def hand_on(dz, dx):
        q = at(z + n_z - dz, x + n_x - dx)
        block = rows.at[span(q)]
        return push(block, block, hand_ssem.at[dz * n_x + dx], row_rsem.at[q], place(twin))

    hand_on(0, 0).start()
    order = [0, 1, 3, 2]
    for dz in order:
        for dx in order:
            if dz or dx:
                row_copy(dz, dx).start()

    def id_copy(i):
        return push(ids.at[me], ids.at[me], id_ssem.at[i], id_rsem.at[me], place(ring(i)))

    each(n_plane, lambda i: id_copy(i).start())

    def cast_step(j, carry):
        c0 = pl.multiple_of(j * load_cols, load_cols)
        odd = lax.rem(j, 2) * 2
        load(student_hbm, j, odd).wait()
        ws[:, pl.ds(c0, load_cols)] = stage[odd].astype(BF16)

        @pl.when(j + 2 < n_load)
        def _():
            load(student_hbm, j + 2, odd).start()

        load(teacher_hbm, j, odd + 1).wait()
        wt[:, pl.ds(c0, load_cols)] = stage[odd + 1].astype(BF16)

        @pl.when(j + 2 < n_load)
        def _():
            load(teacher_hbm, j + 2, odd + 1).start()

        return carry

    lax.fori_loop(0, n_load, cast_step, 0)

    def take_direct(dz, skip_own=False):
        for dx in order:
            if not (skip_own and dx == 0):
                row_arrival(at(z + n_z - dz, x + n_x - dx)).wait_recv()
                hand_on(dz, dx).start()

    def take_handed(dz):
        for dx in order:
            row_arrival(at(z + n_z - dz, x + n_x - dx) + 1 - 2 * core).wait_recv()

    take_direct(0, skip_own=True)
    take_handed(0)

    cols_one = 512
    n_one = cols // cols_one

    def lse_copy(k_at, i):
        return push(
            lse_send.at[k_at], lse_all.at[k_at, me], lse_ssem.at[k_at, i], lse_rsem.at[k_at, me], place(ring(i))
        )

    def chunk_step(k, carry):
        dz = k + (k // 2) * (1 - 2 * lax.rem(k, 2))
        after = k + 1
        dz_after = after + (after // 2) * (1 - 2 * lax.rem(after, 2))
        z_at = lax.rem(z + n_z - dz, n_z)
        for peak, total in ((peak_s, sum_s), (peak_t, sum_t)):
            peak[...] = jnp.full(peak.shape, LOWEST, F32)
            total[...] = jnp.zeros(total.shape, F32)

        def first_step(j, inner):
            c0 = pl.multiple_of(j * cols_one, cols_one)
            for r in range(chunk // row_chunk):
                part = slice(r * row_chunk, (r + 1) * row_chunk)
                here = pl.ds(pl.multiple_of(z_at * chunk + r * row_chunk, row_chunk), row_chunk)
                for e0, w, peak, total, scale, shift in (
                    (0, ws, peak_s, sum_s, SCALE_S, False),
                    (emb, wt, peak_t, sum_t, SCALE_T, True),
                ):
                    logit = jnp.dot(
                        rows[here, e0 : e0 + emb], w[:, pl.ds(c0, cols_one)], preferred_element_type=F32
                    )
                    if shift:
                        logit = logit - centre[:, pl.ds(pl.multiple_of(first_col + c0, cols_one), cols_one)]
                    pieces = [logit[:, n * LANES : (n + 1) * LANES] for n in range(cols_one // LANES)]
                    before = peak[part, :]
                    now = before
                    for piece in pieces:
                        now = jnp.maximum(now, piece)
                    acc = total[part, :] * jnp.exp2((before - now) * scale)
                    for piece in pieces:
                        acc = acc + jnp.exp2((piece - now) * scale)
                    total[part, :] = acc
                    peak[part, :] = now
            return inner

        lax.fori_loop(0, n_one // 2, first_step, 0)

        @pl.when(after < n_z)
        def _():
            take_direct(dz_after)

        lax.fori_loop(n_one // 2, n_one, first_step, 0)

        for n, (peak, total, scale) in enumerate(((peak_s, sum_s, SCALE_S), (peak_t, sum_t, SCALE_T))):
            for g in range(tiles):
                part = slice(g * LANES, (g + 1) * LANES)
                lanes_peak = peak[part, :]
                top = jnp.max(lanes_peak, axis=1, keepdims=True)
                mass = jnp.sum(total[part, :] * jnp.exp2((lanes_peak - top) * scale), axis=1, keepdims=True)
                r = n * tiles + g
                lse_tile[r : r + 1, :] = to_row(top * scale + jnp.log(mass) * LOG2E)
        lse_send[z_at] = lse_tile[...]
        lse_all[z_at, me] = lse_tile[...]
        each(n_plane, lambda i: lse_copy(z_at, i).start())

        @pl.when(after < n_z)
        def _():
            take_handed(dz_after)

        return carry

    lax.fori_loop(0, n_z, chunk_step, 0)

    rows_across[...] = rows[:, :emb].T
    unit_acc[...] = jnp.zeros(unit_acc.shape, F32)

    each(n_plane, lambda i: push(
        ids.at[back(i)], ids.at[back(i)], id_ssem.at[i], id_rsem.at[back(i)], place(twin)
    ).wait_recv())
    lane = iota((1, LANES), 1)
    row_ratio = float(mask_count * PATCH_IMG // patch_count)
    for half in range(HALVES):
        id_rows = []
        for g in range(half * group_tiles, (half + 1) * group_tiles):
            id_rows.append(jnp.where(lane < mask_count, ids[2 * g], ids[2 * g + 1]))
        id_tile = jnp.concatenate(id_rows, axis=0)
        weight = jnp.zeros_like(id_tile)
        for label in range(IMG_GROUP):
            hits = jnp.where(id_tile == float(label), 1.0, 0.0)
            count = jnp.sum(jnp.sum(hits, axis=0, keepdims=True), axis=1, keepdims=True)
            weight = weight + hits * (row_ratio / jnp.maximum(count, 1.0))
        weight_tile[half * group_tiles : (half + 1) * group_tiles, :] = weight

    loss_acc[...] = jnp.zeros(loss_acc.shape, F32)
    for z_at in range(n_z):
        each(n_plane, lambda i: push(
            lse_send.at[z_at], lse_all.at[z_at, back(i)], lse_ssem.at[z_at, i], lse_rsem.at[z_at, back(i)], place(twin)
        ).wait_recv())
        top = lse_all[z_at, 0]
        for q in range(1, n_plane):
            top = jnp.maximum(top, lse_all[z_at, q])
        mass = jnp.exp2(lse_all[z_at, 0] - top)
        for q in range(1, n_plane):
            mass = mass + jnp.exp2(lse_all[z_at, q] - top)
        lse = top + jnp.log(mass) * LOG2E
        weight = weight_tile[z_at * tiles : (z_at + 1) * tiles, :]
        gain = jnp.log(weight / student_temp) * LOG2E
        lse_tile[:tiles, :] = lse[:tiles] - gain
        lse_tile[tiles:, :] = lse[tiles:] - gain
        loss_acc[:tiles, :] += weight * lse[:tiles] * LN2
        for g in range(tiles):
            part = slice(z_at * chunk + g * LANES, z_at * chunk + (g + 1) * LANES)
            shift_s[part, :] = jnp.broadcast_to(to_column(lse_tile[g : g + 1, :]), (LANES, LANES))
            shift_t[part, :] = jnp.broadcast_to(to_column(lse_tile[tiles + g : tiles + g + 1, :]), (LANES, LANES))

    cols_two = 512
    rows_two = 512
    n_two = cols // cols_two
    lag = 2
    loss_send[...] = jnp.zeros(loss_send.shape, F32)
    partner = (HALVES * y + 1 - zh, p)

    def block_at(j):
        return pl.ds(pl.multiple_of(j * cols_two, cols_two), cols_two)

    def slab_copy(j, i):
        to = lax.rem(y + i, n_y)
        return push(
            slab_send.at[to, :, block_at(j)],
            slab_recv.at[y, :, block_at(j)],
            slab_ssem.at[i, j],
            slab_rsem.at[y, j],
            y_peer(i),
        )

    def slab_arrival(j, i):
        origin = lax.rem(y + n_y - i, n_y)
        return push(
            slab_send.at[y, :, block_at(j)],
            slab_recv.at[origin, :, block_at(j)],
            slab_ssem.at[i, j],
            slab_rsem.at[origin, j],
            partner,
        )

    def half_copy(j):
        return push(half_send.at[:, block_at(j)], half_recv.at[:, block_at(j)], half_ssem.at[j], half_rsem.at[j], partner)

    n_chips = n_plane // 2

    def twin_copy(chip):
        block = span(2 * chip + 1 - core)
        return push(unit_send.at[block], twin_recv.at[chip], twin_ssem.at[chip], twin_rsem.at[chip], place(twin))

    def unit_copy(chip):
        q = 2 * chip + core
        return push(
            unit_send.at[span(q)], unit_recv.at[me // 2], unit_ssem.at[chip], unit_rsem.at[me // 2], place(q)
        )

    def merge(index, chips, own_plane):
        for n in range(chips):
            chip = index * chips + n
            twin_copy(chip).wait_recv()
            block = span(2 * chip + core)
            both_terms = unit_send[block, :].astype(F32) + twin_recv[chip].astype(F32)
            unit_send[block, :] = both_terms.astype(BF16)
            if own_plane:

                @pl.when(chip != me // 2)
                def _():
                    unit_copy(chip).start()
            else:
                unit_copy(chip).start()

    def settle(j):
        block = block_at(j)
        for i in range(1, n_y):
            slab_arrival(j, i).wait_recv()
        acc = slab_send[y, :, block].astype(F32)
        for i in range(1, n_y):
            acc = acc + slab_recv[lax.rem(y + n_y - i, n_y), :, block].astype(F32)
        both[...] = acc.reshape(HALVES, part_rows, cols_two)
        proto_grad_out[:, pl.ds(pl.multiple_of(first_col + j * cols_two, cols_two), cols_two)] = both[zh]
        half_send[:, block] = both[1 - zh].astype(BF16)
        half_copy(j).start()

    def second_block(j, last):
        block = block_at(j)
        w_block = ws[:, block]
        wt_block = wt[:, block]
        shift = centre[:, pl.ds(pl.multiple_of(first_col + j * cols_two, cols_two), cols_two)] * SCALE_T
        acc = jnp.zeros((emb, cols_two), F32)
        cross = jnp.zeros((rows_two, LANES), F32)
        n_parts = n_rows // rows_two
        owners = rows_two // mask_count
        for r in range(n_parts):
            index = lax.rem(r + 1 + me // owners, n_parts) if last else r
            part = pl.ds(pl.multiple_of(index * rows_two, rows_two), rows_two)
            zs = jnp.dot(rows[part, :emb], w_block, preferred_element_type=F32)
            zt = jnp.dot(rows[part, emb:], wt_block, preferred_element_type=F32)
            a = shift_s[part, :]
            b = shift_t[part, :]
            pieces = []
            for n in range(cols_two // LANES):
                cut = slice(n * LANES, (n + 1) * LANES)
                logit = zs[:, cut]
                target = jnp.exp2(zt[:, cut] * SCALE_T - (b + shift[:, cut]))
                pieces.append((jnp.exp2(logit * SCALE_S - a) - target).astype(BF16))
                cross = cross + target * logit
            glog = jnp.concatenate(pieces, axis=1)
            product = lax.dot_general(glog, w_block, (((1,), (1,)), ((), ())), preferred_element_type=F32)
            acc = acc + jnp.dot(rows_across[:, part], glog, preferred_element_type=F32)
            if last:
                unit_send[part, :] = (unit_acc[part, :] + product).astype(BF16)
                for n in range(owners // 2):
                    twin_copy(index * (owners // 2) + n).start()
                if r > 0:
                    merge(lax.rem(r + me // owners, n_parts), owners // 2, False)
            else:
                unit_acc[part, :] += product
        slab_send[:, :, block] = acc.astype(BF16).reshape(n_y, slab, cols_two)
        loss_send[...] += jnp.sum(jnp.sum(cross.reshape(rows_two // 8, 8, LANES), axis=0), axis=0, keepdims=True)
        for i in range(1, n_y):
            slab_copy(j, i).start()

    def second_step(j, carry):
        second_block(j, False)

        @pl.when(j >= lag)
        def _():
            settle(j - lag)

        return carry

    lax.fori_loop(0, n_two - 1, second_step, 0)
    second_block(n_two - 1, True)

    plane_devices = rows_two // mask_count
    merge(me // plane_devices, plane_devices // 2, True)
    unit_recv[me // 2] = unit_send[span(me), :]

    loss_recv[me] = loss_send[...]

    def loss_copy(i):
        return push(loss_send, loss_recv.at[me], loss_ssem.at[i], loss_rsem.at[me], place(ring(i)))

    each(n_plane, lambda i: loss_copy(i).start())
    settle(n_two - 1 - lag)
    settle(n_two - lag)

    each(n_plane, lambda i: push(
        loss_send, loss_recv.at[back(i)], loss_ssem.at[i], loss_rsem.at[back(i)], place(twin)
    ).wait_recv())
    cross_total = loss_recv[0]
    for q in range(1, n_plane):
        cross_total = cross_total + loss_recv[q]
    group_recv[y] = jnp.sum(loss_acc[...], axis=0, keepdims=True) - cross_total

    def group_copy(i):
        return push(group_recv.at[y], group_recv.at[y], group_ssem.at[i], group_rsem.at[y], y_peer(i))

    for i in range(1, n_y):
        group_copy(i).start()

    settle(n_two - 1)

    def unit_take(i):
        chip = lax.rem(me // 2 + n_chips - i, n_chips)
        push(
            unit_send.at[span(me)], unit_recv.at[chip], unit_ssem.at[i], unit_rsem.at[chip], place(twin)
        ).wait_recv()

    each(n_chips, unit_take)
    unit_grad = unit_recv[0].astype(F32)
    for chip in range(1, n_chips):
        unit_grad = unit_grad + unit_recv[chip].astype(F32)
    raw = raw_keep[...]
    inv = inv_keep[:, 0:1]
    dotted = jnp.sum(raw * unit_grad, axis=1, keepdims=True)
    row_grad_out[...] = inv * unit_grad - (inv * inv * inv) * raw * dotted

    for i in range(1, n_y):
        q = lax.rem(y + n_y - i, n_y)
        push(group_recv.at[y], group_recv.at[q], group_ssem.at[i], group_rsem.at[q], partner).wait_recv()
    total = group_recv[0]
    for q in range(1, n_y):
        total = total + group_recv[q]
    loss_out[0, 0] = jnp.sum(total) * (1.0 / float(n_rows * n_y))

    other_col = (1 - zh) * cols
    for j in range(n_two):
        half_copy(j).wait_recv()
        to = pl.ds(pl.multiple_of(other_col + j * cols_two, cols_two), cols_two)
        proto_grad_out[:, to] = half_recv[:, j * cols_two : (j + 1) * cols_two].astype(F32)

    for dz in order:
        for dx in order:
            if dz or dx:
                row_copy(dz, dx).wait_send()
            hand_on(dz, dx).wait_send()

    def sent(i):
        id_copy(i).wait_send()
        loss_copy(i).wait_send()
        for z_at in range(n_z):
            lse_copy(z_at, i).wait_send()

    each(n_plane, sent)
    for chip in range(n_chips):
        twin_copy(chip).wait_send()

        @pl.when(chip != me // 2)
        def _():
            unit_copy(chip).wait_send()

    for j in range(n_two):
        half_copy(j).wait_send()
        for i in range(1, n_y):
            slab_copy(j, i).wait_send()
    for i in range(1, n_y):
        group_copy(i).wait_send()


def head(n_dp, n_proto, student_patch, teacher_patch, patch_image, masked_rows, student_proto, teacher_proto, centre):
    mask_count = masked_rows.shape[1]
    emb, all_cols = student_proto.shape
    cols = all_cols // HALVES
    n_plane = n_proto * HALVES
    n_y = n_dp // HALVES
    n_z = 2 * HALVES
    n_rows = mask_count * n_plane
    chunk = n_rows // n_z
    vmem = pl.BlockSpec(memory_space=pltpu.VMEM)
    hbm = pl.BlockSpec(memory_space=pl.ANY)
    dma = pltpu.SemaphoreType.DMA
    slab = emb // n_y
    blocks = cols // 512
    return pl.pallas_call(
        functools.partial(head_kernel, n_dp, n_proto),
        out_shape=(
            jax.ShapeDtypeStruct((mask_count, emb), F32),
            jax.ShapeDtypeStruct((slab // HALVES, all_cols), F32),
            jax.ShapeDtypeStruct((1, 1), F32),
        ),
        in_specs=[hbm] * 7,
        out_specs=(vmem, vmem, pl.BlockSpec(memory_space=pltpu.SMEM)),
        scratch_shapes=[
            pltpu.VMEM(student_patch.shape, BF16),
            pltpu.VMEM(teacher_patch.shape, BF16),
            pltpu.VMEM(patch_image.shape, jnp.int32),
            pltpu.VMEM(masked_rows.shape, jnp.int32),
            pltpu.VMEM(centre.shape, F32),
            pltpu.VMEM((4, emb, 1024), F32),
            pltpu.VMEM((emb, cols), BF16),
            pltpu.VMEM((emb, cols), BF16),
            pltpu.VMEM((n_rows, 2 * emb), BF16),
            pltpu.VMEM((emb, n_rows), BF16),
            pltpu.VMEM((mask_count, emb), F32),
            pltpu.VMEM((mask_count, LANES), F32),
            pltpu.VMEM((n_plane, 1, LANES), F32),
            pltpu.VMEM((chunk, LANES), F32),
            pltpu.VMEM((chunk, LANES), F32),
            pltpu.VMEM((chunk, LANES), F32),
            pltpu.VMEM((chunk, LANES), F32),
            pltpu.VMEM((n_rows, LANES), F32),
            pltpu.VMEM((n_rows, LANES), F32),
            pltpu.VMEM((n_rows // LANES, LANES), F32),
            pltpu.VMEM((8, LANES), F32),
            pltpu.VMEM((n_z, 8, LANES), F32),
            pltpu.VMEM((n_z, n_plane, 8, LANES), F32),
            pltpu.VMEM((n_rows, emb), F32),
            pltpu.VMEM((n_rows, emb), BF16),
            pltpu.VMEM((n_plane // 2, mask_count, emb), BF16),
            pltpu.VMEM((n_plane // 2, mask_count, emb), BF16),
            pltpu.VMEM((n_y, slab, cols), BF16),
            pltpu.VMEM((n_y, slab, cols), BF16),
            pltpu.VMEM((HALVES, slab // HALVES, 512), F32),
            pltpu.VMEM((slab // HALVES, cols), BF16),
            pltpu.VMEM((slab // HALVES, cols), BF16),
            pltpu.VMEM((8, LANES), F32),
            pltpu.VMEM((1, LANES), F32),
            pltpu.VMEM((n_plane, 1, LANES), F32),
            pltpu.VMEM((n_y, 1, LANES), F32),
            dma((5,)),
            dma((4,)),
            dma((n_plane // 2,)),
            dma((n_plane // 2,)),
            dma((n_plane,)),
            dma((n_plane,)),
            dma((n_plane,)),
            dma((n_z, n_plane)),
            dma((n_z, n_plane)),
            dma((n_plane // 2,)),
            dma((n_plane // 2,)),
            dma((n_plane // 2,)),
            dma((n_plane // 2,)),
            dma((n_y, blocks)),
            dma((n_y, blocks)),
            dma((blocks,)),
            dma((blocks,)),
            dma((n_plane,)),
            dma((n_plane,)),
            dma((n_y,)),
            dma((n_y,)),
        ],
        compiler_params=pltpu.CompilerParams(
            collective_id=0, has_side_effects=True, vmem_limit_bytes=56 * 1024 * 1024
        ),
        name="head",
    )(student_patch, teacher_patch, patch_image, masked_rows, student_proto, teacher_proto, centre)


def local(
    student_patch,
    teacher_patch,
    patch_image,
    masked_rows,
    student_proto,
    teacher_proto,
    first_moment,
    second_moment,
    centre,
):
    n_proto = lax.axis_size("proto")
    n_dp = lax.axis_size("dp")
    row_grad, proto_grad, loss = head(
        n_dp,
        n_proto,
        student_patch[0],
        teacher_patch[0],
        patch_image,
        masked_rows,
        student_proto,
        teacher_proto,
        centre[None, :],
    )
    slab_rows = first_moment.shape[0]
    slab_start = lax.axis_index("dp") * slab_rows
    own_student = lax.dynamic_slice_in_dim(student_proto, slab_start, slab_rows, 0)
    own_teacher = lax.dynamic_slice_in_dim(teacher_proto, slab_start, slab_rows, 0)
    new_first = beta_one * first_moment + (1.0 - beta_one) * proto_grad
    new_second = beta_two * second_moment + (1.0 - beta_two) * proto_grad * proto_grad
    step_size = new_first / fix_one / (jnp.sqrt(new_second / fix_two) + 1e-08)
    new_student = own_student - learn_rate * (step_size + decay_rate * own_student)
    new_teacher = teacher_keep * own_teacher + (1.0 - teacher_keep) * new_student
    return (row_grad[None], new_student, new_first, new_second, new_teacher, loss[0, 0])


def solution(mesh):
    in_specs = (
        P("dp", "proto", None),
        P("dp", "proto", None),
        P("dp", "proto"),
        P("dp", "proto"),
        P(None, "proto"),
        P(None, "proto"),
        P("dp", "proto"),
        P("dp", "proto"),
        P("proto"),
    )
    out_specs = (
        P("dp", "proto", None),
        P("dp", "proto"),
        P("dp", "proto"),
        P("dp", "proto"),
        P("dp", "proto"),
        P(),
    )
    return jax.shard_map(local, mesh=mesh, in_specs=in_specs, out_specs=out_specs, check_vma=False)
```

```python
import functools
import math

import jax
import jax.numpy as jnp
from jax import lax
from jax.experimental import pallas as pl
from jax.experimental.pallas import tpu as pltpu
from jax.sharding import PartitionSpec as P

PATCH_IMG = 256
IMG_GROUP = 8

student_temp = 0.1
teacher_temp = 0.07
beta_one = 0.9
beta_two = 0.999
fix_one = 0.9999734386011124
fix_two = 0.09520785288629038
learn_rate = 0.002
decay_rate = 0.04
teacher_keep = 0.994

F32 = jnp.float32
BF16 = jnp.bfloat16
MESH = pl.DeviceIdType.MESH
LOG2E = math.log2(math.e)
LN2 = math.log(2.0)
SCALE_S = LOG2E / student_temp
SCALE_T = LOG2E / teacher_temp
LOWEST = -3.0e38
LANES = 128
SMALLEST = 1.0e-25
LARGEST = 1.0e30
HALVES = 2


def iota(shape, axis):
    return lax.broadcasted_iota(jnp.int32, shape, axis)


def eye(n):
    return iota((n, n), 0) == iota((n, n), 1)


def to_column(row):
    n = row.shape[1]
    return jnp.sum(jnp.where(eye(n), jnp.broadcast_to(row, (n, n)), 0.0), axis=1, keepdims=True)


def to_row(column):
    n = column.shape[0]
    return jnp.sum(jnp.where(eye(n), jnp.broadcast_to(column, (n, n)), 0.0), axis=0, keepdims=True)


def head_kernel(
    guarded,
    n_dp,
    n_proto,
    student_patch_hbm,
    teacher_patch_hbm,
    patch_image_hbm,
    masked_rows_hbm,
    student_hbm,
    teacher_hbm,
    centre_hbm,
    row_grad_out,
    proto_grad_out,
    loss_out,
    student_patch,
    teacher_patch,
    patch_image,
    masked_rows,
    centre,
    stage,
    ws,
    wt,
    rows,
    rows_across,
    raw_keep,
    inv_keep,
    ids,
    peak_s,
    sum_s,
    peak_t,
    sum_t,
    shift_s,
    shift_t,
    weight_tile,
    lse_tile,
    lse_send,
    lse_all,
    unit_acc,
    unit_send,
    unit_recv,
    twin_recv,
    slab_send,
    slab_recv,
    both,
    half_send,
    half_recv,
    loss_acc,
    loss_send,
    loss_recv,
    group_recv,
    input_sem,
    stage_sem,
    row_ssem,
    hand_ssem,
    row_rsem,
    id_ssem,
    id_rsem,
    lse_ssem,
    lse_rsem,
    unit_ssem,
    unit_rsem,
    twin_ssem,
    twin_rsem,
    slab_ssem,
    slab_rsem,
    half_ssem,
    half_rsem,
    loss_ssem,
    loss_rsem,
    group_ssem,
    group_rsem,
):
    n_y = n_dp // HALVES
    n_plane = HALVES * n_proto
    n_z = 2 * HALVES
    n_x = n_plane // (2 * n_z)
    d = lax.axis_index("dp")
    p = lax.axis_index("proto")
    y = d // HALVES
    zh = lax.rem(d, HALVES)
    me = zh * n_proto + p
    z = me // (2 * n_x)
    x = lax.rem(me // 2, n_x)
    core = lax.rem(p, 2)
    twin = me + 1 - 2 * core
    mask_count = masked_rows.shape[1]
    patch_count = patch_image.shape[1]
    emb, cols = ws.shape
    n_rows = rows.shape[0]
    chunk = n_rows // n_z
    slab = emb // n_y
    part_rows = slab // HALVES
    load_cols = stage.shape[2]
    row_chunk = 256
    tiles = chunk // LANES
    group_tiles = n_rows // LANES // HALVES
    first_col = zh * cols

    def place(q):
        return (HALVES * y + q // n_proto, lax.rem(q, n_proto))

    def ring(i):
        return lax.rem(me + i, n_plane)

    def back(i):
        return lax.rem(me + n_plane - i, n_plane)

    def push(src, dst, ssem, rsem, target):
        return pltpu.make_async_remote_copy(
            src_ref=src, dst_ref=dst, send_sem=ssem, recv_sem=rsem, device_id=target, device_id_type=MESH
        )

    def each(count, body):
        def step(i, carry):
            body(i)
            return carry

        lax.fori_loop(1, count, step, 0)

    inputs = []
    for n, (src, dst) in enumerate(
        (
            (masked_rows_hbm, masked_rows),
            (student_patch_hbm, student_patch),
            (teacher_patch_hbm, teacher_patch),
            (patch_image_hbm, patch_image),
            (centre_hbm, centre),
        )
    ):
        inputs.append(pltpu.make_async_copy(src, dst, input_sem.at[n]))
        inputs[-1].start()

    barrier = pltpu.get_barrier_semaphore()

    def y_peer(i):
        return (HALVES * lax.rem(y + i, n_y) + zh, p)

    each(n_plane, lambda i: pl.semaphore_signal(barrier, inc=1, device_id=place(ring(i)), device_id_type=MESH))
    each(n_y, lambda i: pl.semaphore_signal(barrier, inc=1, device_id=y_peer(i), device_id_type=MESH))

    n_load = cols // load_cols

    def load(hbm, j, slot):
        c0 = pl.multiple_of(first_col + j * load_cols, load_cols)
        return pltpu.make_async_copy(hbm.at[:, pl.ds(c0, load_cols)], stage.at[slot], stage_sem.at[slot])

    load(student_hbm, 0, 0).start()
    load(teacher_hbm, 0, 1).start()
    load(student_hbm, 1, 2).start()
    load(teacher_hbm, 1, 3).start()

    for copy in inputs:
        copy.wait()
    picked = to_column(masked_rows[...].astype(F32))
    one_hot = iota((mask_count, patch_count), 1).astype(F32) == picked
    one_hot_f = jnp.where(one_hot, 1.0, 0.0)
    one_hot_b = one_hot_f.astype(BF16)
    raw_s = jnp.dot(one_hot_b, student_patch[...], preferred_element_type=F32)
    raw_t = jnp.dot(one_hot_b, teacher_patch[...], preferred_element_type=F32)
    inv_s = lax.rsqrt(jnp.sum(raw_s * raw_s, axis=1, keepdims=True) + 1e-06)
    inv_t = lax.rsqrt(jnp.sum(raw_t * raw_t, axis=1, keepdims=True) + 1e-06)

    def span(q):
        return pl.ds(pl.multiple_of(q * mask_count, mask_count), mask_count)

    rows[span(me), :emb] = (raw_s * inv_s).astype(BF16)
    rows[span(me), emb:] = (raw_t * inv_t).astype(BF16)
    raw_keep[...] = raw_s
    inv_keep[...] = jnp.broadcast_to(inv_s, inv_keep.shape)
    own_ids = to_row(jnp.sum(one_hot_f * patch_image[...].astype(F32), axis=1, keepdims=True))
    ids[me] = jnp.concatenate([own_ids, own_ids], axis=1)

    pl.semaphore_wait(barrier, n_plane + n_y - 2)

    def at(z_at, x_at):
        return (lax.rem(z_at, n_z) * n_x + lax.rem(x_at, n_x)) * 2 + core

    def row_copy(dz, dx):
        i = dz * n_x + dx
        block = rows.at[span(me)]
        return push(block, block, row_ssem.at[i], row_rsem.at[me], place(at(z + dz, x + dx)))

    def row_arrival(q):
        block = rows.at[span(q)]
        return push(block, block, row_ssem.at[0], row_rsem.at[q], place(twin))

    def hand_on(dz, dx):
        q = at(z + n_z - dz, x + n_x - dx)
        block = rows.at[span(q)]
        return push(block, block, hand_ssem.at[dz * n_x + dx], row_rsem.at[q], place(twin))

    hand_on(0, 0).start()
    order = [0, 1, 3, 2]
    for dz in order:
        for dx in order:
            if dz or dx:
                row_copy(dz, dx).start()

    def id_copy(i):
        return push(ids.at[me], ids.at[me], id_ssem.at[i], id_rsem.at[me], place(ring(i)))

    each(n_plane, lambda i: id_copy(i).start())

    def cast_step(j, carry):
        c0 = pl.multiple_of(j * load_cols, load_cols)
        odd = lax.rem(j, 2) * 2
        load(student_hbm, j, odd).wait()
        ws[:, pl.ds(c0, load_cols)] = stage[odd].astype(BF16)

        @pl.when(j + 2 < n_load)
        def _():
            load(student_hbm, j + 2, odd).start()

        load(teacher_hbm, j, odd + 1).wait()
        wt[:, pl.ds(c0, load_cols)] = stage[odd + 1].astype(BF16)

        @pl.when(j + 2 < n_load)
        def _():
            load(teacher_hbm, j + 2, odd + 1).start()

        return carry

    lax.fori_loop(0, n_load, cast_step, 0)

    def take_direct(dz, skip_own=False):
        for dx in order:
            if not (skip_own and dx == 0):
                row_arrival(at(z + n_z - dz, x + n_x - dx)).wait_recv()
                hand_on(dz, dx).start()

    def take_handed(dz):
        for dx in order:
            row_arrival(at(z + n_z - dz, x + n_x - dx) + 1 - 2 * core).wait_recv()

    take_direct(0, skip_own=True)
    take_handed(0)

    cols_one = 512 if guarded else 2048
    n_one = cols // cols_one

    def lse_copy(k_at, i):
        return push(
            lse_send.at[k_at], lse_all.at[k_at, me], lse_ssem.at[k_at, i], lse_rsem.at[k_at, me], place(ring(i))
        )

    def chunk_step(k, carry):
        dz = k + (k // 2) * (1 - 2 * lax.rem(k, 2))
        after = k + 1
        dz_after = after + (after // 2) * (1 - 2 * lax.rem(after, 2))
        z_at = lax.rem(z + n_z - dz, n_z)
        for peak, total in ((peak_s, sum_s), (peak_t, sum_t)):
            peak[...] = jnp.full(peak.shape, LOWEST, F32)
            total[...] = jnp.zeros(total.shape, F32)

        def first_step(j, inner):
            c0 = pl.multiple_of(j * cols_one, cols_one)
            for r in range(chunk // row_chunk):
                part = slice(r * row_chunk, (r + 1) * row_chunk)
                here = pl.ds(pl.multiple_of(z_at * chunk + r * row_chunk, row_chunk), row_chunk)
                for e0, w, peak, total, scale, shift in (
                    (0, ws, peak_s, sum_s, SCALE_S, False),
                    (emb, wt, peak_t, sum_t, SCALE_T, True),
                ):
                    logit = jnp.dot(
                        rows[here, e0 : e0 + emb], w[:, pl.ds(c0, cols_one)], preferred_element_type=F32
                    )
                    if not guarded:
                        acc = total[part, :]
                        for n in range(cols_one // LANES):
                            power = logit[:, n * LANES : (n + 1) * LANES] * scale
                            if shift:
                                at_col = pl.multiple_of(first_col + c0 + n * LANES, LANES)
                                power = power - centre[:, pl.ds(at_col, LANES)] * scale
                            acc = acc + jnp.exp2(power)
                        total[part, :] = acc
                        continue
                    if shift:
                        logit = logit - centre[:, pl.ds(pl.multiple_of(first_col + c0, cols_one), cols_one)]
                    pieces = [logit[:, n * LANES : (n + 1) * LANES] for n in range(cols_one // LANES)]
                    before = peak[part, :]
                    now = before
                    for piece in pieces:
                        now = jnp.maximum(now, piece)
                    acc = total[part, :] * jnp.exp2((before - now) * scale)
                    for piece in pieces:
                        acc = acc + jnp.exp2((piece - now) * scale)
                    total[part, :] = acc
                    peak[part, :] = now
            return inner

        lax.fori_loop(0, n_one // 2, first_step, 0)

        @pl.when(after < n_z)
        def _():
            take_direct(dz_after)

        lax.fori_loop(n_one // 2, n_one, first_step, 0)

        for n, (peak, total, scale) in enumerate(((peak_s, sum_s, SCALE_S), (peak_t, sum_t, SCALE_T))):
            for g in range(tiles):
                part = slice(g * LANES, (g + 1) * LANES)
                if not guarded:
                    mass = jnp.sum(total[part, :], axis=1, keepdims=True)
                    usable = jnp.logical_and(mass > SMALLEST, mass < LARGEST)
                    r = n * tiles + g
                    lse_tile[r : r + 1, :] = to_row(jnp.where(usable, jnp.log(mass) * LOG2E, jnp.nan))
                    continue
                lanes_peak = peak[part, :]
                top = jnp.max(lanes_peak, axis=1, keepdims=True)
                mass = jnp.sum(total[part, :] * jnp.exp2((lanes_peak - top) * scale), axis=1, keepdims=True)
                r = n * tiles + g
                lse_tile[r : r + 1, :] = to_row(top * scale + jnp.log(mass) * LOG2E)
        lse_send[z_at] = lse_tile[...]
        lse_all[z_at, me] = lse_tile[...]
        each(n_plane, lambda i: lse_copy(z_at, i).start())

        @pl.when(after < n_z)
        def _():
            take_handed(dz_after)

        return carry

    lax.fori_loop(0, n_z, chunk_step, 0)

    rows_across[...] = rows[:, :emb].T
    unit_acc[...] = jnp.zeros(unit_acc.shape, F32)

    each(n_plane, lambda i: push(
        ids.at[back(i)], ids.at[back(i)], id_ssem.at[i], id_rsem.at[back(i)], place(twin)
    ).wait_recv())
    lane = iota((1, LANES), 1)
    row_ratio = float(mask_count * PATCH_IMG // patch_count)
    for half in range(HALVES):
        id_rows = []
        for g in range(half * group_tiles, (half + 1) * group_tiles):
            id_rows.append(jnp.where(lane < mask_count, ids[2 * g], ids[2 * g + 1]))
        id_tile = jnp.concatenate(id_rows, axis=0)
        weight = jnp.zeros_like(id_tile)
        for label in range(IMG_GROUP):
            hits = jnp.where(id_tile == float(label), 1.0, 0.0)
            count = jnp.sum(jnp.sum(hits, axis=0, keepdims=True), axis=1, keepdims=True)
            weight = weight + hits * (row_ratio / jnp.maximum(count, 1.0))
        weight_tile[half * group_tiles : (half + 1) * group_tiles, :] = weight

    loss_acc[...] = jnp.zeros(loss_acc.shape, F32)
    for z_at in range(n_z):
        each(n_plane, lambda i: push(
            lse_send.at[z_at], lse_all.at[z_at, back(i)], lse_ssem.at[z_at, i], lse_rsem.at[z_at, back(i)], place(twin)
        ).wait_recv())
        top = lse_all[z_at, 0]
        for q in range(1, n_plane):
            top = jnp.maximum(top, lse_all[z_at, q])
        mass = jnp.exp2(lse_all[z_at, 0] - top)
        for q in range(1, n_plane):
            mass = mass + jnp.exp2(lse_all[z_at, q] - top)
        lse = top + jnp.log(mass) * LOG2E
        weight = weight_tile[z_at * tiles : (z_at + 1) * tiles, :]
        gain = jnp.log(weight / student_temp) * LOG2E
        lse_tile[:tiles, :] = lse[:tiles] - gain
        lse_tile[tiles:, :] = lse[tiles:] - gain
        loss_acc[:tiles, :] += weight * lse[:tiles] * LN2
        for g in range(tiles):
            part = slice(z_at * chunk + g * LANES, z_at * chunk + (g + 1) * LANES)
            shift_s[part, :] = jnp.broadcast_to(to_column(lse_tile[g : g + 1, :]), (LANES, LANES))
            shift_t[part, :] = jnp.broadcast_to(to_column(lse_tile[tiles + g : tiles + g + 1, :]), (LANES, LANES))

    cols_two = 512
    rows_two = 512
    n_two = cols // cols_two
    lag = 2
    loss_send[...] = jnp.zeros(loss_send.shape, F32)
    partner = (HALVES * y + 1 - zh, p)

    def block_at(j):
        return pl.ds(pl.multiple_of(j * cols_two, cols_two), cols_two)

    def slab_copy(j, i):
        to = lax.rem(y + i, n_y)
        return push(
            slab_send.at[to, :, block_at(j)],
            slab_recv.at[y, :, block_at(j)],
            slab_ssem.at[i, j],
            slab_rsem.at[y, j],
            y_peer(i),
        )

    def slab_arrival(j, i):
        origin = lax.rem(y + n_y - i, n_y)
        return push(
            slab_send.at[y, :, block_at(j)],
            slab_recv.at[origin, :, block_at(j)],
            slab_ssem.at[i, j],
            slab_rsem.at[origin, j],
            partner,
        )

    def half_copy(j):
        return push(half_send.at[:, block_at(j)], half_recv.at[:, block_at(j)], half_ssem.at[j], half_rsem.at[j], partner)

    n_chips = n_plane // 2

    def twin_copy(chip):
        block = span(2 * chip + 1 - core)
        return push(unit_send.at[block], twin_recv.at[chip], twin_ssem.at[chip], twin_rsem.at[chip], place(twin))

    def unit_copy(chip):
        q = 2 * chip + core
        return push(
            unit_send.at[span(q)], unit_recv.at[me // 2], unit_ssem.at[chip], unit_rsem.at[me // 2], place(q)
        )

    def merge(index, chips, own_plane):
        for n in range(chips):
            chip = index * chips + n
            twin_copy(chip).wait_recv()
            block = span(2 * chip + core)
            both_terms = unit_send[block, :].astype(F32) + twin_recv[chip].astype(F32)
            unit_send[block, :] = both_terms.astype(BF16)
            if own_plane:

                @pl.when(chip != me // 2)
                def _():
                    unit_copy(chip).start()
            else:
                unit_copy(chip).start()

    def settle(j):
        block = block_at(j)
        for i in range(1, n_y):
            slab_arrival(j, i).wait_recv()
        acc = slab_send[y, :, block].astype(F32)
        for i in range(1, n_y):
            acc = acc + slab_recv[lax.rem(y + n_y - i, n_y), :, block].astype(F32)
        both[...] = acc.reshape(HALVES, part_rows, cols_two)
        proto_grad_out[:, pl.ds(pl.multiple_of(first_col + j * cols_two, cols_two), cols_two)] = both[zh]
        half_send[:, block] = both[1 - zh].astype(BF16)
        half_copy(j).start()

    def second_block(j, last):
        block = block_at(j)
        w_block = ws[:, block]
        wt_block = wt[:, block]
        shift = centre[:, pl.ds(pl.multiple_of(first_col + j * cols_two, cols_two), cols_two)] * SCALE_T
        acc = jnp.zeros((emb, cols_two), F32)
        cross = jnp.zeros((rows_two, LANES), F32)
        n_parts = n_rows // rows_two
        owners = rows_two // mask_count
        for r in range(n_parts):
            index = lax.rem(r + 1 + me // owners, n_parts) if last else r
            part = pl.ds(pl.multiple_of(index * rows_two, rows_two), rows_two)
            zs = jnp.dot(rows[part, :emb], w_block, preferred_element_type=F32)
            zt = jnp.dot(rows[part, emb:], wt_block, preferred_element_type=F32)
            a = shift_s[part, :]
            b = shift_t[part, :]
            pieces = []
            for n in range(cols_two // LANES):
                cut = slice(n * LANES, (n + 1) * LANES)
                logit = zs[:, cut]
                target = jnp.exp2(zt[:, cut] * SCALE_T - (b + shift[:, cut]))
                pieces.append((jnp.exp2(logit * SCALE_S - a) - target).astype(BF16))
                cross = cross + target * logit
            glog = jnp.concatenate(pieces, axis=1)
            product = lax.dot_general(glog, w_block, (((1,), (1,)), ((), ())), preferred_element_type=F32)
            acc = acc + jnp.dot(rows_across[:, part], glog, preferred_element_type=F32)
            if last:
                unit_send[part, :] = (unit_acc[part, :] + product).astype(BF16)
                for n in range(owners // 2):
                    twin_copy(index * (owners // 2) + n).start()
                if r > 0:
                    merge(lax.rem(r + me // owners, n_parts), owners // 2, False)
            else:
                unit_acc[part, :] += product
        slab_send[:, :, block] = acc.astype(BF16).reshape(n_y, slab, cols_two)
        loss_send[...] += jnp.sum(jnp.sum(cross.reshape(rows_two // 8, 8, LANES), axis=0), axis=0, keepdims=True)
        for i in range(1, n_y):
            slab_copy(j, i).start()

    def second_step(j, carry):
        second_block(j, False)

        @pl.when(j >= lag)
        def _():
            settle(j - lag)

        return carry

    lax.fori_loop(0, n_two - 1, second_step, 0)
    second_block(n_two - 1, True)

    plane_devices = rows_two // mask_count
    merge(me // plane_devices, plane_devices // 2, True)
    unit_recv[me // 2] = unit_send[span(me), :]

    loss_recv[me] = loss_send[...]

    def loss_copy(i):
        return push(loss_send, loss_recv.at[me], loss_ssem.at[i], loss_rsem.at[me], place(ring(i)))

    each(n_plane, lambda i: loss_copy(i).start())
    settle(n_two - 1 - lag)
    settle(n_two - lag)

    each(n_plane, lambda i: push(
        loss_send, loss_recv.at[back(i)], loss_ssem.at[i], loss_rsem.at[back(i)], place(twin)
    ).wait_recv())
    cross_total = loss_recv[0]
    for q in range(1, n_plane):
        cross_total = cross_total + loss_recv[q]
    group_recv[y] = jnp.sum(loss_acc[...], axis=0, keepdims=True) - cross_total

    def group_copy(i):
        return push(group_recv.at[y], group_recv.at[y], group_ssem.at[i], group_rsem.at[y], y_peer(i))

    for i in range(1, n_y):
        group_copy(i).start()

    settle(n_two - 1)

    def unit_take(i):
        chip = lax.rem(me // 2 + n_chips - i, n_chips)
        push(
            unit_send.at[span(me)], unit_recv.at[chip], unit_ssem.at[i], unit_rsem.at[chip], place(twin)
        ).wait_recv()

    each(n_chips, unit_take)
    unit_grad = unit_recv[0].astype(F32)
    for chip in range(1, n_chips):
        unit_grad = unit_grad + unit_recv[chip].astype(F32)
    raw = raw_keep[...]
    inv = inv_keep[:, 0:1]
    dotted = jnp.sum(raw * unit_grad, axis=1, keepdims=True)
    row_grad_out[...] = inv * unit_grad - (inv * inv * inv) * raw * dotted

    for i in range(1, n_y):
        q = lax.rem(y + n_y - i, n_y)
        push(group_recv.at[y], group_recv.at[q], group_ssem.at[i], group_rsem.at[q], partner).wait_recv()
    total = group_recv[0]
    for q in range(1, n_y):
        total = total + group_recv[q]
    loss_out[0, 0] = jnp.sum(total) * (1.0 / float(n_rows * n_y))

    other_col = (1 - zh) * cols
    for j in range(n_two):
        half_copy(j).wait_recv()
        to = pl.ds(pl.multiple_of(other_col + j * cols_two, cols_two), cols_two)
        proto_grad_out[:, to] = half_recv[:, j * cols_two : (j + 1) * cols_two].astype(F32)

    for dz in order:
        for dx in order:
            if dz or dx:
                row_copy(dz, dx).wait_send()
            hand_on(dz, dx).wait_send()

    def sent(i):
        id_copy(i).wait_send()
        loss_copy(i).wait_send()
        for z_at in range(n_z):
            lse_copy(z_at, i).wait_send()

    each(n_plane, sent)
    for chip in range(n_chips):
        twin_copy(chip).wait_send()

        @pl.when(chip != me // 2)
        def _():
            unit_copy(chip).wait_send()

    for j in range(n_two):
        half_copy(j).wait_send()
        for i in range(1, n_y):
            slab_copy(j, i).wait_send()
    for i in range(1, n_y):
        group_copy(i).wait_send()


def head(guarded, n_dp, n_proto, student_patch, teacher_patch, patch_image, masked_rows, student_proto, teacher_proto, centre):
    mask_count = masked_rows.shape[1]
    emb, all_cols = student_proto.shape
    cols = all_cols // HALVES
    n_plane = n_proto * HALVES
    n_y = n_dp // HALVES
    n_z = 2 * HALVES
    n_rows = mask_count * n_plane
    chunk = n_rows // n_z
    vmem = pl.BlockSpec(memory_space=pltpu.VMEM)
    hbm = pl.BlockSpec(memory_space=pl.ANY)
    dma = pltpu.SemaphoreType.DMA
    slab = emb // n_y
    blocks = cols // 512
    return pl.pallas_call(
        functools.partial(head_kernel, guarded, n_dp, n_proto),
        out_shape=(
            jax.ShapeDtypeStruct((mask_count, emb), F32),
            jax.ShapeDtypeStruct((slab // HALVES, all_cols), F32),
            jax.ShapeDtypeStruct((1, 1), F32),
        ),
        in_specs=[hbm] * 7,
        out_specs=(vmem, vmem, pl.BlockSpec(memory_space=pltpu.SMEM)),
        scratch_shapes=[
            pltpu.VMEM(student_patch.shape, BF16),
            pltpu.VMEM(teacher_patch.shape, BF16),
            pltpu.VMEM(patch_image.shape, jnp.int32),
            pltpu.VMEM(masked_rows.shape, jnp.int32),
            pltpu.VMEM(centre.shape, F32),
            pltpu.VMEM((4, emb, 1024), F32),
            pltpu.VMEM((emb, cols), BF16),
            pltpu.VMEM((emb, cols), BF16),
            pltpu.VMEM((n_rows, 2 * emb), BF16),
            pltpu.VMEM((emb, n_rows), BF16),
            pltpu.VMEM((mask_count, emb), F32),
            pltpu.VMEM((mask_count, LANES), F32),
            pltpu.VMEM((n_plane, 1, LANES), F32),
            pltpu.VMEM((chunk, LANES), F32),
            pltpu.VMEM((chunk, LANES), F32),
            pltpu.VMEM((chunk, LANES), F32),
            pltpu.VMEM((chunk, LANES), F32),
            pltpu.VMEM((n_rows, LANES), F32),
            pltpu.VMEM((n_rows, LANES), F32),
            pltpu.VMEM((n_rows // LANES, LANES), F32),
            pltpu.VMEM((8, LANES), F32),
            pltpu.VMEM((n_z, 8, LANES), F32),
            pltpu.VMEM((n_z, n_plane, 8, LANES), F32),
            pltpu.VMEM((n_rows, emb), F32),
            pltpu.VMEM((n_rows, emb), BF16),
            pltpu.VMEM((n_plane // 2, mask_count, emb), BF16),
            pltpu.VMEM((n_plane // 2, mask_count, emb), BF16),
            pltpu.VMEM((n_y, slab, cols), BF16),
            pltpu.VMEM((n_y, slab, cols), BF16),
            pltpu.VMEM((HALVES, slab // HALVES, 512), F32),
            pltpu.VMEM((slab // HALVES, cols), BF16),
            pltpu.VMEM((slab // HALVES, cols), BF16),
            pltpu.VMEM((8, LANES), F32),
            pltpu.VMEM((1, LANES), F32),
            pltpu.VMEM((n_plane, 1, LANES), F32),
            pltpu.VMEM((n_y, 1, LANES), F32),
            dma((5,)),
            dma((4,)),
            dma((n_plane // 2,)),
            dma((n_plane // 2,)),
            dma((n_plane,)),
            dma((n_plane,)),
            dma((n_plane,)),
            dma((n_z, n_plane)),
            dma((n_z, n_plane)),
            dma((n_plane // 2,)),
            dma((n_plane // 2,)),
            dma((n_plane // 2,)),
            dma((n_plane // 2,)),
            dma((n_y, blocks)),
            dma((n_y, blocks)),
            dma((blocks,)),
            dma((blocks,)),
            dma((n_plane,)),
            dma((n_plane,)),
            dma((n_y,)),
            dma((n_y,)),
        ],
        compiler_params=pltpu.CompilerParams(
            collective_id=int(guarded), has_side_effects=True, vmem_limit_bytes=56 * 1024 * 1024
        ),
        name="head_guarded" if guarded else "head",
    )(student_patch, teacher_patch, patch_image, masked_rows, student_proto, teacher_proto, centre)


def local(
    student_patch,
    teacher_patch,
    patch_image,
    masked_rows,
    student_proto,
    teacher_proto,
    first_moment,
    second_moment,
    centre,
):
    n_proto = lax.axis_size("proto")
    n_dp = lax.axis_size("dp")
    operands = (
        student_patch[0],
        teacher_patch[0],
        patch_image,
        masked_rows,
        student_proto,
        teacher_proto,
        centre[None, :],
    )
    quick = head(False, n_dp, n_proto, *operands)
    row_grad, proto_grad, loss = lax.cond(
        jnp.isnan(quick[2][0, 0]), lambda: head(True, n_dp, n_proto, *operands), lambda: quick
    )
    slab_rows = first_moment.shape[0]
    slab_start = lax.axis_index("dp") * slab_rows
    own_student = lax.dynamic_slice_in_dim(student_proto, slab_start, slab_rows, 0)
    own_teacher = lax.dynamic_slice_in_dim(teacher_proto, slab_start, slab_rows, 0)
    new_first = beta_one * first_moment + (1.0 - beta_one) * proto_grad
    new_second = beta_two * second_moment + (1.0 - beta_two) * proto_grad * proto_grad
    step_size = new_first / fix_one / (jnp.sqrt(new_second / fix_two) + 1e-08)
    new_student = own_student - learn_rate * (step_size + decay_rate * own_student)
    new_teacher = teacher_keep * own_teacher + (1.0 - teacher_keep) * new_student
    return (row_grad[None], new_student, new_first, new_second, new_teacher, loss[0, 0])


def solution(mesh):
    in_specs = (
        P("dp", "proto", None),
        P("dp", "proto", None),
        P("dp", "proto"),
        P("dp", "proto"),
        P(None, "proto"),
        P(None, "proto"),
        P("dp", "proto"),
        P("dp", "proto"),
        P("proto"),
    )
    out_specs = (
        P("dp", "proto", None),
        P("dp", "proto"),
        P("dp", "proto"),
        P("dp", "proto"),
        P("dp", "proto"),
        P(),
    )
    return jax.shard_map(local, mesh=mesh, in_specs=in_specs, out_specs=out_specs, check_vma=False)
```
